32 devices in a mesh: section: 2 (over core), cin: 4 (over y, x), cout: 4 (over z).
Axes of the slice: x: 2, y: 2, z: 4, core: 2. Of those that a mesh axis runs over, the one named last changes fastest.
Arguments:
- inner_features: bfloat16 [2, 784, 2560], P('section', None, ('cin', 'cout')), may hold values from 0 to 2
- block_input: bfloat16 [2, 784, 5120], P('section', None, ('cin', 'cout')), may hold values from -6 to 6
- first_kernel: bfloat16 [9, 2560, 2560], P(None, 'cin', 'cout'), may hold values from -0.0546875 to 0.0546875
- expand_weight: bfloat16 [2560, 5120], P('cout', 'cin'), may hold values from -0.15625 to 0.15625
- reduce_weight: bfloat16 [5120, 5120], P(('cin', 'section'), 'cout'), may hold values from -0.125 to 0.125
- stride_kernel: bfloat16 [9, 5120, 5120], P(None, 'cout', ('section', 'cin')), may hold values from -0.0390625 to 0.0390625
- output_grad: bfloat16 [2, 196, 5120], P(None, None, ('section', 'cin', 'cout')), may hold values from -6 to 6
Outputs:
- inner_gradient: float32 [2, 784, 2560], P('section', None, ('cin', 'cout'))
- input_gradient: bfloat16 [2, 784, 5120], P('section', None, ('cin', 'cout'))
- first_gradient: float32 [9, 2560, 2560], P(None, 'cin', 'cout')
- expand_gradient: float32 [2560, 5120], P('cout', 'cin')
- reduce_gradient: float32 [5120, 5120], P(('cin', 'section'), 'cout')
- stride_gradient: float32 [9, 5120, 5120], P(None, 'cout', ('section', 'cin'))
The draws below stay inside these ranges and needn't reach their ends.
All inputs are finite; a program needn't handle non-finite values.
Results may differ from the reference program's by a relative error of at most 0.013.
Values may be sent and summed in bfloat16 or wider, within the bound.
No kernel may reach another device: no remote copies, remote signals or barrier semaphores. Data moves between devices by JAX's collectives and lax.ppermute only.
A program may use at most 256 MiB of HBM per device.

```python
import jax
import jax.numpy as jnp
from jax import lax

INA = 2560
OUTA = 5120
INB = 5120
SIDE = 28
IMAGES = 2
HW = 784
HH = 196


def raised(values, own_key, source, target, blocks, factor):
    def block_of(axis_at):
        return (jnp.arange(values.shape[axis_at]) // (values.shape[axis_at] // blocks)).reshape((-1,) + (1,) * (values.ndim - 1 - axis_at))

    near = jax.random.permutation(own_key, blocks)[block_of(target)]
    other_side = (block_of(target) + blocks // 2) % blocks
    return jnp.where((block_of(source) == near) | (block_of(source) == other_side), factor * values, values)


def shard_levels(rng, extent, shards, low, top_value):
    gain = 1.0
    for axis_at, parts in shards:
        heights = jax.random.uniform(jax.random.fold_in(jax.random.fold_in(rng, 6), axis_at), (parts,), jnp.float32, low / len(shards), top_value / len(shards))
        gain = gain * jnp.repeat(jnp.exp(heights), extent[axis_at] // parts).reshape((-1,) + (1,) * (len(extent) - 1 - axis_at))
    return gain


def gaussian(own_key, shape, spread, bound, pieces=(), kind=jnp.bfloat16):
    values = jax.random.normal(own_key, shape, jnp.float32) * spread
    if len(pieces) > 0:
        values = shard_levels(own_key, shape, pieces, -0.22, 0.18) * values
    return jnp.clip(values, min=-bound, max=bound).astype(kind)


def bell_draw_with(own_key, dims, deviation, bound, split, heavy, kind=jnp.bfloat16):
    drawn = deviation * jax.random.normal(own_key, dims, jnp.float32)
    if split:
        drawn = drawn * shard_levels(own_key, dims, split, -0.22, 0.18)
    return jnp.clip(raised(drawn, jax.random.fold_in(own_key, 3), *heavy), -bound, bound).astype(kind)


def setup_inputs(seed: int = 0) -> dict:
    splits = jax.random.split(jax.random.key(seed), 8)
    inner_features = jnp.clip(2.0 * jax.random.uniform(splits[0], (IMAGES, HW, INA), jnp.float32) ** shard_levels(splits[0], (IMAGES, HW, INA), ((0, 2), (2, 16)), -0.2, 0.2), 0.0, 2.0).astype(jnp.bfloat16)
    block_input = gaussian(splits[1], (IMAGES, HW, OUTA), 1.0, 6.0, ((0, 2), (2, 16)))
    first_kernel = bell_draw_with(splits[2], (9, INA, INA), (9 * INA) ** -0.5, 0.0546875, ((1, 4), (2, 4)), (1, 2, 4, 2.0))
    expand_weight = bell_draw_with(splits[3], (INA, OUTA), INA ** -0.5, 0.15625, ((0, 4), (1, 4)), (0, 1, 4, 2.0))
    reduce_weight = bell_draw_with(splits[4], (OUTA, INB), OUTA ** -0.5, 0.125, ((0, 8), (1, 4)), (0, 1, 8, 2.0))
    stride_kernel = bell_draw_with(splits[5], (9, INB, INB), (9 * INB) ** -0.5, 0.0390625, ((1, 4), (2, 8)), (2, 1, 8, 2.0))
    output_grad = gaussian(splits[6], (IMAGES, HH, INB), 1.0, 6.0, ((2, 32),))
    return {"inner_features": inner_features, "block_input": block_input, "first_kernel": first_kernel, "expand_weight": expand_weight, "reduce_weight": reduce_weight, "stride_kernel": stride_kernel, "output_grad": output_grad}


def smooth_gate(values):
    return values * jax.nn.sigmoid(values)


def gate_slope(values):
    logistic = jax.nn.sigmoid(values)
    return logistic * (1.0 + values * (1.0 - logistic))


def flatten_rows(images):
    return images.reshape(images.shape[0] * images.shape[1], images.shape[2])


def project(images, matrix):
    product = jnp.dot(flatten_rows(images), matrix, preferred_element_type=jnp.float32)
    return product.reshape(images.shape[0], images.shape[1], matrix.shape[1])


def project_back(grads, matrix):
    product = lax.dot_general(flatten_rows(grads), matrix, (((1,), (1,)), ((), ())), preferred_element_type=jnp.float32)
    return product.reshape(grads.shape[0], grads.shape[1], matrix.shape[0])


def outer_rows(left, right):
    return lax.dot_general(flatten_rows(left), flatten_rows(right), (((0,), (0,)), ((), ())), preferred_element_type=jnp.float32)


def padded_grid(images, side):
    grid = images.reshape(images.shape[0], side, side, images.shape[2])
    return jnp.pad(grid, ((0, 0), (1, 1), (1, 1), (0, 0)))


def conv_same(images, kernel, side):
    padded = padded_grid(images, side)
    total = jnp.zeros((images.shape[0] * side * side, kernel.shape[2]), jnp.float32)
    for row in range(3):
        for column in range(3):
            window = padded[:, row:row + side, column:column + side, :].reshape(-1, images.shape[2])
            total = total + jnp.dot(window, kernel[3 * row + column], preferred_element_type=jnp.float32)
    return total.reshape(images.shape[0], side * side, kernel.shape[2])


def conv_same_back(grads, kernel, side):
    padded = padded_grid(grads, side)
    total = jnp.zeros((grads.shape[0] * side * side, kernel.shape[1]), jnp.float32)
    for row in range(3):
        for column in range(3):
            window = padded[:, 2 - row:2 - row + side, 2 - column:2 - column + side, :].reshape(-1, grads.shape[2])
            total = total + lax.dot_general(window, kernel[3 * row + column], (((1,), (1,)), ((), ())), preferred_element_type=jnp.float32)
    return total.reshape(grads.shape[0], side * side, kernel.shape[1])


def conv_same_weight(images, grads, side):
    padded = padded_grid(images, side)
    flat = flatten_rows(grads)
    terms = []
    for row in range(3):
        for column in range(3):
            window = padded[:, row:row + side, column:column + side, :].reshape(-1, images.shape[2])
            terms.append(lax.dot_general(window, flat, (((0,), (0,)), ((), ())), preferred_element_type=jnp.float32))
    return jnp.stack(terms)


def conv_half_back(grads, kernel, side):
    half = side // 2
    count = grads.shape[0]
    flat = flatten_rows(grads)
    canvas = None
    for row in range(3):
        for column in range(3):
            term = lax.dot_general(flat, kernel[3 * row + column], (((1,), (1,)), ((), ())), preferred_element_type=jnp.float32)
            term = term.reshape(count, half, half, kernel.shape[1])
            placed = lax.pad(term, jnp.zeros((), term.dtype), ((0, 0, 0), (row, 3 - row, 1), (column, 3 - column, 1), (0, 0, 0)))
            canvas = placed if canvas is None else canvas + placed
    return canvas[:, 1:side + 1, 1:side + 1, :].reshape(count, side * side, kernel.shape[1])


def conv_half_weight(images, grads, side):
    padded = padded_grid(images, side)
    flat = flatten_rows(grads)
    terms = []
    for row in range(3):
        for column in range(3):
            window = padded[:, row:row + side:2, column:column + side:2, :].reshape(-1, images.shape[2])
            terms.append(lax.dot_general(window, flat, (((0,), (0,)), ((), ())), preferred_element_type=jnp.float32))
    return jnp.stack(terms)


def reference(inner_features, block_input, first_kernel, expand_weight, reduce_weight, stride_kernel, output_grad):
    first_hidden = conv_same(inner_features, first_kernel, SIDE)
    first_act = smooth_gate(first_hidden).astype(jnp.bfloat16)
    expanded = project(first_act, expand_weight)
    joined_pre = block_input.astype(jnp.float32) + expanded
    joined = smooth_gate(joined_pre).astype(jnp.bfloat16)
    second_hidden = project(joined, reduce_weight)
    second_act = smooth_gate(second_hidden).astype(jnp.bfloat16)
    back_second = conv_half_back(output_grad, stride_kernel, SIDE)
    stride_gradient = conv_half_weight(second_act, output_grad, SIDE)
    masked_second = (back_second * gate_slope(second_hidden)).astype(jnp.bfloat16)
    reduce_gradient = outer_rows(joined, masked_second)
    back_joined = project_back(masked_second, reduce_weight)
    input_gradient = (back_joined * gate_slope(joined_pre)).astype(jnp.bfloat16)
    expand_gradient = outer_rows(first_act, input_gradient)
    back_first = project_back(input_gradient, expand_weight)
    masked_first = (back_first * gate_slope(first_hidden)).astype(jnp.bfloat16)
    inner_gradient = conv_same_back(masked_first, first_kernel, SIDE)
    first_gradient = conv_same_weight(inner_features, masked_first, SIDE)
    return (inner_gradient, input_gradient, first_gradient, expand_gradient, reduce_gradient, stride_gradient)
```

```python
import functools

import jax
import jax.numpy as jnp
from jax import lax
from jax.experimental import pallas as pl
from jax.experimental.pallas import tpu as pltpu
from jax.sharding import PartitionSpec as P

SIDE = 28
TAPS = 9
F32 = jnp.float32
BF16 = jnp.bfloat16
NN = (((1,), (0,)), ((), ()))
TN = (((0,), (0,)), ((), ()))
NT = (((1,), (1,)), ((), ()))


def smooth_gate(values):
    return values * jax.nn.sigmoid(values)


def gate_slope(values):
    logistic = jax.nn.sigmoid(values)
    return logistic * (1.0 + values * (1.0 - logistic))


def dot(left, right, dims):
    return lax.dot_general(left, right, dims, preferred_element_type=F32)


def lanes_of(count):
    return -(-count // 128) * 128


def params():
    return pltpu.CompilerParams(
        dimension_semantics=("arbitrary",), vmem_limit_bytes=56 * 1024 * 1024
    )


def cost(flops, moved):
    return pl.CostEstimate(flops=flops, bytes_accessed=moved, transcendentals=0)


def fill_columns(planes, image, side):
    rows, pixels = image.shape
    wide = planes.shape[2]
    column = lax.broadcasted_iota(jnp.int32, (rows, pixels), 1) % side
    zero = jnp.zeros_like(image)
    planes[0, :, :pixels] = jnp.where(column == side - 1, zero, image)
    planes[1, :, :pixels] = image
    planes[2, :, :pixels] = jnp.where(column == 0, zero, image)
    if wide > pixels:
        for k in range(3):
            planes[k, :, pixels:] = jnp.zeros((rows, wide - pixels), image.dtype)


def read_shifted(planes, dy, dx, side):
    wide = planes.shape[2]
    amount = (2 * wide - (side * dy + dx)) % wide
    return pltpu.roll(planes[dx + 1], amount, 1)


def partner(index, k, n):
    return index ^ k if n & (n - 1) == 0 else (index + k) % n


def source(index, k, n):
    return index ^ k if n & (n - 1) == 0 else (index + n - k) % n


def whole(shape):
    return pl.BlockSpec(shape, lambda *_: (0,) * len(shape))


def one_step(body, ins, outs, scratch, flops):
    moved = sum(v.size * v.dtype.itemsize for v in ins)
    moved += sum(v.size * v.dtype.itemsize for v in outs)
    return pl.pallas_call(
        body,
        out_shape=outs,
        in_specs=[pl.BlockSpec(memory_space=pltpu.VMEM)] * len(ins),
        out_specs=[pl.BlockSpec(memory_space=pltpu.VMEM)] * len(outs),
        scratch_shapes=scratch,
        compiler_params=pltpu.CompilerParams(vmem_limit_bytes=56 * 1024 * 1024),
        cost_estimate=cost(flops, moved),
    )(*ins)


def like(shape, dtype=BF16):
    return jax.ShapeDtypeStruct(shape, dtype)


def held_type(size):
    return BF16 if size % 16 == 0 else F32


def rows_at(index, size):
    return pl.ds(pl.multiple_of(index * size, 8), size)


def write_chunks(outs, total, me, n):
    size = outs[0].shape[0]
    for k in range(n):
        rows = rows_at(partner(me, k, n), size)
        outs[k][...] = total[rows, : outs[k].shape[1]].astype(BF16)


def conv_forward_body(x_ref, w_ref, *rest, side, n):
    outs, (planes, total) = rest[:n], rest[n:]
    t = pl.program_id(0)
    me = lax.axis_index("cin")

    @pl.when(t == 0)
    def _():
        fill_columns(planes, x_ref[...], side)
        total[...] = jnp.zeros_like(total)

    window = read_shifted(planes, t // 3 - 1, t % 3 - 1, side)
    total[...] += dot(w_ref[0], window, TN)

    @pl.when(t == TAPS - 1)
    def _():
        write_chunks(outs, total, me, n)


def conv_forward(x, kernel, side, n):
    depth, pixels = x.shape
    width = kernel.shape[2]
    wide = lanes_of(pixels + side + 1)
    return pl.pallas_call(
        functools.partial(conv_forward_body, side=side, n=n),
        out_shape=[like((width // n, pixels))] * n,
        grid=(TAPS,),
        in_specs=[
            whole((depth, pixels)),
            pl.BlockSpec((1, depth, width), lambda t: (t, 0, 0)),
        ],
        out_specs=[whole((width // n, pixels))] * n,
        scratch_shapes=[
            pltpu.VMEM((3, depth, wide), BF16),
            pltpu.VMEM((width, wide), F32),
        ],
        compiler_params=params(),
        cost_estimate=cost(2 * TAPS * depth * width * pixels, 2 * kernel.size + 4 * x.size),
    )(x, kernel)


def conv_back_body(m_ref, w_ref, *rest, side, n):
    outs, (planes, total) = rest[:n], rest[n:]
    t = pl.program_id(0)
    me = lax.axis_index("cout")

    @pl.when(t == 0)
    def _():
        fill_columns(planes, m_ref[...], side)
        total[...] = jnp.zeros_like(total)

    window = read_shifted(planes, 1 - t // 3, 1 - t % 3, side)
    total[...] += dot(w_ref[0], window, NN)

    @pl.when(t == TAPS - 1)
    def _():
        write_chunks(outs, total, me, n)


def conv_back(m, kernel, side, n):
    width, pixels = m.shape
    depth = kernel.shape[1]
    wide = lanes_of(pixels + side + 1)
    return pl.pallas_call(
        functools.partial(conv_back_body, side=side, n=n),
        out_shape=[like((depth // n, pixels))] * n,
        grid=(TAPS,),
        in_specs=[
            whole((width, pixels)),
            pl.BlockSpec((1, depth, width), lambda t: (t, 0, 0)),
        ],
        out_specs=[whole((depth // n, pixels))] * n,
        scratch_shapes=[
            pltpu.VMEM((3, width, wide), BF16),
            pltpu.VMEM((depth, wide), F32),
        ],
        compiler_params=params(),
        cost_estimate=cost(2 * TAPS * depth * width * pixels, 2 * kernel.size + 4 * m.size),
    )(m, kernel)


def conv_weight_body(xa_ref, xb_ref, ma_ref, mb_ref, o_ref, pa, pb, ga, gb, *, side):
    t = pl.program_id(0)
    pixels = ma_ref.shape[1]

    @pl.when(t == 0)
    def _():
        fill_columns(pa, xa_ref[...], side)
        fill_columns(pb, xb_ref[...], side)
        ga[...] = jnp.zeros_like(ga)
        gb[...] = jnp.zeros_like(gb)
        ga[:, :pixels] = ma_ref[...]
        gb[:, :pixels] = mb_ref[...]

    dy, dx = t // 3 - 1, t % 3 - 1
    o_ref[0] = dot(read_shifted(pa, dy, dx, side), ga[...], NT) + dot(
        read_shifted(pb, dy, dx, side), gb[...], NT
    )


def conv_weight(xa, xb, ma, mb, side):
    depth, pixels = xa.shape
    width = ma.shape[0]
    wide = lanes_of(pixels + side + 1)
    return pl.pallas_call(
        functools.partial(conv_weight_body, side=side),
        out_shape=jax.ShapeDtypeStruct((TAPS, depth, width), F32),
        grid=(TAPS,),
        in_specs=[pl.BlockSpec((depth, pixels), lambda t: (0, 0))] * 2
        + [pl.BlockSpec((width, pixels), lambda t: (0, 0))] * 2,
        out_specs=pl.BlockSpec((1, depth, width), lambda t: (t, 0, 0)),
        scratch_shapes=[pltpu.VMEM((3, depth, wide), BF16)] * 2
        + [pltpu.VMEM((width, wide), BF16)] * 2,
        compiler_params=params(),
        cost_estimate=cost(4 * TAPS * depth * width * pixels, 4 * TAPS * depth * width),
    )(xa, xb, ma, mb)


def fill_moved(moved, cots, half):
    count, rows, pixels = cots.shape
    wide = moved.shape[2] // count
    column = lax.broadcasted_iota(jnp.int32, (rows, wide), 1) % half
    for b in range(count):
        moved[0, :, b * wide : (b + 1) * wide] = jnp.zeros((rows, wide), moved.dtype)
        moved[0, :, b * wide : b * wide + pixels] = cots[b]
        image = moved[0, :, b * wide : (b + 1) * wide]
        inner = jnp.where(column == 0, jnp.zeros_like(image), image)
        moved[1, :, b * wide : (b + 1) * wide] = pltpu.roll(inner, wide - 1, 1)
        moved[2, :, b * wide : (b + 1) * wide] = pltpu.roll(image, wide - half, 1)
        moved[3, :, b * wide : (b + 1) * wide] = pltpu.roll(inner, wide - half - 1, 1)


def chosen(plane, small, large, side):
    half = side // 2
    i = lax.broadcasted_iota(jnp.int32, (small, large), 0)
    q = lax.broadcasted_iota(jnp.int32, (small, large), 1)
    row, column = i // half, i % half
    pixel = (2 * row + plane // 2) * side + 2 * column + plane % 2
    hit = (q == pixel) & (i < half * half)
    return jnp.where(hit, 1.0, 0.0).astype(BF16)


def half_back_body(g_ref, w_ref, kept, sent, moved, total, placed, *, side):
    t = pl.program_id(0)
    count = g_ref.shape[0]
    rows, pixels = placed.shape
    half = rows // 2
    wide = moved.shape[2] // count
    core = lax.axis_index("section")

    @pl.when(t == 0)
    def _():
        fill_moved(moved, g_ref[...], side // 2)
        total[...] = jnp.zeros_like(total)

    ty, tx = t // 3, t % 3
    plane = jnp.where(ty == 1, 0, 2) + jnp.where(tx == 1, 0, 1)
    move = jnp.where(ty == 0, 2, 0) + jnp.where(tx == 0, 1, 0)
    total[plane] += dot(w_ref[0], moved[move], NN)

    @pl.when(t == TAPS - 1)
    def _():
        for b in range(count):
            for k in range(4):
                term = dot(
                    total[k, :, b * wide : (b + 1) * wide].astype(BF16),
                    chosen(k, wide, pixels, side),
                    NN,
                )
                placed[...] = term if k == 0 else placed[...] + term
            kept[b * half : (b + 1) * half, :] = placed[rows_at(core, half), :].astype(BF16)
            sent[b * half : (b + 1) * half, :] = placed[rows_at(1 - core, half), :].astype(BF16)


def half_back(cots, kernel, side):
    count, width, small = cots.shape
    depth = kernel.shape[1]
    wide = lanes_of(small + side // 2 + 1)
    pixels = side * side
    out = (count * depth // 2, pixels)
    return pl.pallas_call(
        functools.partial(half_back_body, side=side),
        out_shape=[like(out)] * 2,
        grid=(TAPS,),
        in_specs=[
            whole((count, width, small)),
            pl.BlockSpec((1, depth, width), lambda t: (t, 0, 0)),
        ],
        out_specs=[whole(out)] * 2,
        scratch_shapes=[
            pltpu.VMEM((4, width, count * wide), BF16),
            pltpu.VMEM((4, depth, count * wide), F32),
            pltpu.VMEM((depth, pixels), F32),
        ],
        compiler_params=params(),
        cost_estimate=cost(2 * TAPS * depth * width * count * small * 2, 2 * kernel.size),
    )(cots, kernel)


def half_weight_body(a_ref, b_ref, g_ref, o_ref, moved, planes, *, side):
    t = pl.program_id(0)
    count = g_ref.shape[0]
    half = a_ref.shape[0] // count
    pixels = a_ref.shape[1]
    wide = moved.shape[2] // count
    core = lax.axis_index("section")

    @pl.when(t == 0)
    def _():
        fill_moved(moved, g_ref[...], side // 2)
        for k in range(4):
            pick = chosen(k, wide, pixels, side)
            for ref, place in ((a_ref, core), (b_ref, 1 - core)):
                for b in range(count):
                    planes[k, rows_at(place, half), b * wide : (b + 1) * wide] = dot(
                        ref[b * half : (b + 1) * half, :], pick, NT
                    ).astype(BF16)

    ty, tx = t // 3, t % 3
    plane = jnp.where(ty == 1, 0, 2) + jnp.where(tx == 1, 0, 1)
    move = jnp.where(ty == 0, 2, 0) + jnp.where(tx == 0, 1, 0)
    o_ref[0] = dot(planes[plane], moved[move], NT)


def half_weight(mine, other, cots, side):
    count, width, small = cots.shape
    rows, pixels = mine.shape
    depth = 2 * rows // count
    wide = lanes_of(small + side // 2 + 1)
    return pl.pallas_call(
        functools.partial(half_weight_body, side=side),
        out_shape=like((TAPS, depth, width), F32),
        grid=(TAPS,),
        in_specs=[
            whole((rows, pixels)),
            whole((rows, pixels)),
            whole((count, width, small)),
        ],
        out_specs=pl.BlockSpec((1, depth, width), lambda t: (t, 0, 0)),
        scratch_shapes=[
            pltpu.VMEM((4, width, count * wide), BF16),
            pltpu.VMEM((4, depth, count * wide), BF16),
        ],
        compiler_params=params(),
        cost_estimate=cost(
            2 * TAPS * depth * width * count * small * 2, 4 * TAPS * depth * width
        ),
    )(mine, other, cots)


def expand(first_block, weight, n):
    depth, width = weight.shape
    pixels = first_block.shape[1]

    def body(x_ref, w_ref, *rest):
        outs, total = rest[:n], rest[n]
        total[...] = dot(w_ref[...], x_ref[...], TN)
        write_chunks(outs, total, lax.axis_index("cout"), n)

    return one_step(
        body,
        [first_block, weight],
        [like((width // n, pixels))] * n,
        [pltpu.VMEM((width, pixels), F32)],
        2 * depth * width * pixels,
    )


def round_target(r, core, z, n):
    return z // (n // 2), z ^ r ^ (core * (n // 2))


def round_block(r, core, z, n):
    place = z ^ r
    return lax.rem(place, n // 2), core ^ (place // (n // 2))


def round_pairs(r, n, back):
    pairs = []
    for core in range(2):
        for z in range(n):
            to_core, to_z = round_target(r, core, z, n)
            pair = (core * n + z, to_core * n + to_z)
            pairs.append(pair[::-1] if back else pair)
    return pairs


def round_send(value, r, n, back=False):
    return lax.ppermute(value, ("section", "cout"), round_pairs(r, n, back))


def reduce_forward(parts, weight, n):
    size, pixels = parts[0].shape
    depth, width = weight.shape
    half = width // 2

    def body(*refs):
        ins, w_ref = refs[:n], refs[n]
        joined, kept, sent, total = refs[n + 1 :]
        core, z = lax.axis_index("section"), lax.axis_index("cout")
        for r in range(n):
            block, image = round_block(r, core, z, n)
            joined[image, rows_at(block, size), :] = ins[r][...]
        for image in range(2):
            total[...] = dot(w_ref[...], joined[image], TN)
            span = slice(image * half, (image + 1) * half)
            kept[span, :] = total[rows_at(core, half), :].astype(BF16)
            sent[span, :] = total[rows_at(1 - core, half), :].astype(BF16)

    return one_step(
        body,
        [*parts, weight],
        [like((2, depth, pixels)), like((2 * half, pixels)), like((2 * half, pixels))],
        [pltpu.VMEM((width, pixels), F32)],
        4 * depth * width * pixels,
    )


def add_halves(kept, got, n):
    rows, pixels = kept.shape
    size = rows // 2 // n

    def body(a_ref, b_ref, *rest):
        outs, total = rest[:n], rest[n]
        me = lax.axis_index("cin")
        total[...] = a_ref[...].astype(F32) + b_ref[...].astype(F32)
        for k in range(n):
            for image in range(2):
                start = image * (rows // 2) + partner(me, k, n) * size
                value = total[pl.ds(pl.multiple_of(start, 8), size), :]
                outs[k][image * size : (image + 1) * size, :] = value.astype(BF16)

    return one_step(
        body,
        [kept, got],
        [like((2 * size, pixels))] * n,
        [pltpu.VMEM((rows, pixels), F32)],
        rows * pixels,
    )


def join_pieces(parts, n):
    double, pixels = parts[0].shape
    size = double // 2

    def body(*refs):
        ins, out, held = refs[:n], refs[n], refs[n + 1]
        me = lax.axis_index("cin")
        for k in range(n):
            for image in range(2):
                start = image * n * size + source(me, k, n) * size
                value = ins[k][image * size : (image + 1) * size, :]
                held[pl.ds(pl.multiple_of(start, 8), size), :] = value.astype(held.dtype)
        out[...] = held[...].astype(BF16)

    return one_step(
        body,
        parts,
        [like((n * double, pixels))],
        [pltpu.VMEM((n * double, pixels), held_type(size))],
        double * pixels,
    )[0]


def place_halves(masked, mine, other, core):
    half = mine[0].shape[0]
    for image in range(2):
        masked[image, rows_at(core, half), :] = mine[image][...]
        masked[image, rows_at(1 - core, half), :] = other[image][...]


def reduce_back(mine, other, weight, n):
    depth, width = weight.shape
    pixels = mine[0].shape[1]
    size = depth // (n // 2)

    def body(*refs):
        a, b, w_ref = refs[0:2], refs[2:4], refs[4]
        outs, masked = refs[5 : 5 + n], refs[5 + n]
        core, z = lax.axis_index("section"), lax.axis_index("cout")
        place_halves(masked, a, b, core)
        for r in range(n):
            block, image = round_block(r, core, z, n)
            outs[r][...] = dot(w_ref[rows_at(block, size), :], masked[image], NN).astype(BF16)

    return one_step(
        body,
        [*mine, *other, weight],
        [like((size, pixels))] * n,
        [pltpu.VMEM((2, width, pixels), BF16)],
        4 * depth * width * pixels,
    )


def reduce_weight_gradient(joined, mine, other):
    _, depth, pixels = joined.shape
    width = 2 * mine[0].shape[0]

    def body(j_ref, *refs):
        a, b, out, masked = refs[0:2], refs[2:4], refs[4], refs[5]
        place_halves(masked, a, b, lax.axis_index("section"))
        out[...] = dot(j_ref[0], masked[0], NT) + dot(j_ref[1], masked[1], NT)

    return one_step(
        body,
        [joined, *mine, *other],
        [like((depth, width), F32)],
        [pltpu.VMEM((2, width, pixels), BF16)],
        4 * depth * width * pixels,
    )[0]


def expand_back(parts, weight, m, n):
    size, pixels = parts[0].shape
    depth, width = weight.shape

    def body(*refs):
        ins, w_ref, outs = refs[:n], refs[n], refs[n + 1 : n + 1 + m]
        held, total = refs[n + 1 + m :]
        z = lax.axis_index("cout")
        for k in range(n):
            held[rows_at(source(z, k, n), size), :] = ins[k][...]
        total[...] = dot(w_ref[...], held[...], NN)
        write_chunks(outs, total, lax.axis_index("cin"), m)

    outs = one_step(
        body,
        [*parts, weight],
        [like((depth // m, pixels))] * m + [like((width, pixels))],
        [pltpu.VMEM((depth, pixels), F32)],
        2 * depth * width * pixels,
    )
    return outs[:m], outs[m]


def outer_pair(a, b, c, d):
    depth, pixels = a.shape
    width = b.shape[0]

    def body(a_ref, b_ref, c_ref, d_ref, out):
        out[...] = dot(a_ref[...], b_ref[...], NT) + dot(c_ref[...], d_ref[...], NT)

    return one_step(
        body, [a, b, c, d], [like((depth, width), F32)], [], 4 * depth * width * pixels
    )[0]


def axis_size(name):
    return lax.axis_size(name)


def swap(value):
    return lax.ppermute(value, "section", [(0, 1), (1, 0)])


def hold(*groups):
    return lax.optimization_barrier(groups)


def exchange(parts, name):
    n = len(parts)
    return [parts[0]] + [
        lax.ppermute(parts[k], name, [(i, partner(i, k, n)) for i in range(n)])
        for k in range(1, n)
    ]


def spread(shard, name):
    return exchange([shard] * axis_size(name), name)


def add_up(parts):
    total = parts[0].astype(F32)
    for part in parts[1:]:
        total = total + part.astype(F32)
    return total


def turn(images):
    return jnp.transpose(images, (0, 2, 1))


def collect(shard, name, axis):
    n = axis_size(name)
    me = lax.axis_index(name)
    size = shard.shape[axis]
    shape = shard.shape[:axis] + (n * size,) + shard.shape[axis + 1 :]
    filled = lax.dynamic_update_slice_in_dim(jnp.zeros(shape, shard.dtype), shard, me * size, axis)
    for k in range(1, n):
        got = lax.ppermute(shard, name, [(i, partner(i, k, n)) for i in range(n)])
        filled = lax.dynamic_update_slice_in_dim(filled, got, source(me, k, n) * size, axis)
    return filled


def gather(shard, name):
    return lax.all_gather(shard, name, axis=0, tiled=True)


def shards(
    inner_features,
    block_input,
    first_kernel,
    expand_weight,
    reduce_weight,
    stride_kernel,
    output_grad,
):
    m, n = axis_size("cin"), axis_size("cout")
    features = turn(inner_features)[0]
    skip = turn(block_input)[0]
    cots = turn(output_grad)

    feature_block = gather(features, "cout")
    feature_block, cots = hold(feature_block, cots)
    cot_block = collect(cots, "cout", 1)
    first_parts = exchange(conv_forward(feature_block, first_kernel, SIDE, m), "cin")
    first_hidden = add_up(first_parts)
    first_act = smooth_gate(first_hidden).astype(BF16)
    first_block = gather(first_act, "cin")

    expand_parts = expand(first_block, expand_weight, n)
    expand_parts, cot_block = hold(expand_parts, cot_block)
    expand_got = exchange(expand_parts, "cout")
    back_kept, back_sent = half_back(cot_block, stride_kernel, SIDE)
    expand_got, back_kept, back_sent = hold(expand_got, back_kept, back_sent)
    joined_pre = skip.astype(F32) + add_up(expand_got)
    joined = smooth_gate(joined_pre).astype(BF16)

    joined_parts = [round_send(joined, r, n) for r in range(n)]
    back_parts = add_halves(back_kept, swap(back_sent), m)
    back_got = exchange(back_parts, "cin")
    joined_parts, back_got = hold(joined_parts, back_got)
    back_piece = add_up(back_got)
    joined_two, hidden_kept, hidden_sent = reduce_forward(joined_parts, reduce_weight, n)
    hidden_parts = add_halves(hidden_kept, swap(hidden_sent), m)
    hidden_piece = add_up(exchange(hidden_parts, "cin"))
    act_piece = smooth_gate(hidden_piece).astype(BF16)
    masked_piece = (back_piece * gate_slope(hidden_piece)).astype(BF16)

    size = masked_piece.shape[0] // 2
    masked_mine = [gather(masked_piece[i * size : (i + 1) * size], "cin") for i in range(2)]
    masked_other = [swap(v) for v in masked_mine]
    back_rounds = reduce_back(masked_mine, masked_other, reduce_weight, n)
    back_rounds, act_piece, joined_two = hold(back_rounds, act_piece, joined_two)
    back_got = [round_send(back_rounds[r], r, n, True) for r in range(n)]
    act_parts = spread(act_piece, "cin")
    reduce_gradient = reduce_weight_gradient(joined_two, masked_mine, masked_other)
    back_got, act_parts, reduce_gradient = hold(back_got, act_parts, reduce_gradient)
    back_joined = add_up(back_got)
    input_gradient = (back_joined * gate_slope(joined_pre)).astype(BF16)

    act_parts, input_gradient = hold(act_parts, input_gradient)
    input_parts = spread(input_gradient, "cout")
    act_mine = join_pieces(act_parts, m)
    stride_gradient = half_weight(act_mine, swap(act_mine), cot_block, SIDE)
    input_parts, stride_gradient = hold(input_parts, stride_gradient)

    first_back, input_wide = expand_back(input_parts, expand_weight, m, n)
    first_back, input_wide, first_block = hold(first_back, input_wide, first_block)
    first_got = exchange(first_back, "cin")
    expand_gradient = outer_pair(first_block, input_wide, swap(first_block), swap(input_wide))
    first_got, expand_gradient = hold(first_got, expand_gradient)
    masked_first = (add_up(first_got) * gate_slope(first_hidden)).astype(BF16)
    masked_block = gather(masked_first, "cin")
    inner_parts = conv_back(masked_block, first_kernel, SIDE, n)
    inner_parts, masked_block, feature_block = hold(inner_parts, masked_block, feature_block)
    inner_got = exchange(inner_parts, "cout")
    first_gradient = conv_weight(
        feature_block, swap(feature_block), masked_block, swap(masked_block), SIDE
    )
    inner_got, first_gradient = hold(inner_got, first_gradient)
    inner_gradient = add_up(inner_got)
    return (
        turn(inner_gradient[None]),
        turn(input_gradient[None]),
        first_gradient,
        expand_gradient,
        reduce_gradient,
        stride_gradient,
    )


def solution(mesh):
    return jax.shard_map(
        shards,
        mesh=mesh,
        in_specs=(
            P("section", None, ("cin", "cout")),
            P("section", None, ("cin", "cout")),
            P(None, "cin", "cout"),
            P("cout", "cin"),
            P(("cin", "section"), "cout"),
            P(None, "cout", ("section", "cin")),
            P(None, None, ("section", "cin", "cout")),
        ),
        out_specs=(
            P("section", None, ("cin", "cout")),
            P("section", None, ("cin", "cout")),
            P(None, "cin", "cout"),
            P("cout", "cin"),
            P(("cin", "section"), "cout"),
            P(None, "cout", ("section", "cin")),
        ),
        check_vma=False,
    )
```

```python
import functools

import jax
import jax.numpy as jnp
from jax import lax
from jax.experimental import pallas as pl
from jax.experimental.pallas import tpu as pltpu
from jax.sharding import PartitionSpec as P

SIDE = 28
TAPS = 9
F32 = jnp.float32
BF16 = jnp.bfloat16
NN = (((1,), (0,)), ((), ()))
TN = (((0,), (0,)), ((), ()))
NT = (((1,), (1,)), ((), ()))


def smooth_gate(values):
    return values * jax.nn.sigmoid(values)


def gate_slope(values):
    logistic = jax.nn.sigmoid(values)
    return logistic * (1.0 + values * (1.0 - logistic))


def dot(left, right, dims):
    return lax.dot_general(left, right, dims, preferred_element_type=F32)


def lanes_of(count):
    return -(-count // 128) * 128


def params():
    return pltpu.CompilerParams(
        dimension_semantics=("arbitrary",), vmem_limit_bytes=56 * 1024 * 1024
    )


def cost(flops, moved):
    return pl.CostEstimate(flops=flops, bytes_accessed=moved, transcendentals=0)


def fill_columns(planes, image, side):
    column = lax.broadcasted_iota(jnp.int32, image.shape, 1) % side
    zero = jnp.zeros_like(image)
    span = image.shape[1]
    planes[0, :, :span] = jnp.where(column == side - 1, zero, image)
    planes[1, :, :span] = image
    planes[2, :, :span] = jnp.where(column == 0, zero, image)
    if planes.shape[2] > span:
        for k in range(3):
            planes[k, :, span:] = jnp.zeros((image.shape[0], planes.shape[2] - span), image.dtype)


def read_shifted(planes, dy, dx, side):
    wide = planes.shape[2]
    amount = (2 * wide - (side * dy + dx)) % wide
    return pltpu.roll(planes[dx + 1], amount, 1)


def partner(index, k, n):
    return index ^ k if n & (n - 1) == 0 else (index + k) % n


def source(index, k, n):
    return index ^ k if n & (n - 1) == 0 else (index + n - k) % n


def whole(shape):
    return pl.BlockSpec(shape, lambda *_: (0,) * len(shape))


def one_step(body, ins, outs, scratch, flops):
    moved = sum(v.size * v.dtype.itemsize for v in ins)
    moved += sum(v.size * v.dtype.itemsize for v in outs)
    return pl.pallas_call(
        body,
        out_shape=outs,
        in_specs=[pl.BlockSpec(memory_space=pltpu.VMEM)] * len(ins),
        out_specs=[pl.BlockSpec(memory_space=pltpu.VMEM)] * len(outs),
        scratch_shapes=scratch,
        compiler_params=pltpu.CompilerParams(vmem_limit_bytes=56 * 1024 * 1024),
        cost_estimate=cost(flops, moved),
    )(*ins)


def like(shape, dtype=BF16):
    return jax.ShapeDtypeStruct(shape, dtype)


def held_type(size):
    return BF16 if size % 16 == 0 else F32


def rows_at(index, size):
    return pl.ds(pl.multiple_of(index * size, 8), size)


def write_chunks(outs, total, me, n, start=0):
    size, width = outs[0].shape
    for k in range(n):
        rows = rows_at(partner(me, k, n), size)
        outs[k][...] = total[rows, start : start + width].astype(BF16)


def spans(wide):
    first = wide // 256 * 128
    return ((0, first), (first, wide))


def stack_row(windows, planes, dy, step, side):
    depth = planes.shape[1]
    for k in range(3):
        windows[k * depth : (k + 1) * depth, :] = read_shifted(planes, dy, step * (k - 1), side)


def conv_forward_body(x_ref, w_ref, *rest, side, n):
    outs, (planes, windows, total) = rest[:-3], rest[-3:]
    t = pl.program_id(0)
    me = lax.axis_index("cin")

    @pl.when(t == 0)
    def _():
        fill_columns(planes, x_ref[...], side)
        total[...] = jnp.zeros_like(total)

    stack_row(windows, planes, t - 1, 1, side)
    total[...] += dot(w_ref[...].reshape(windows.shape[0], w_ref.shape[2]), windows[...], TN)

    @pl.when(t == 2)
    def _():
        pixel = lax.broadcasted_iota(jnp.int32, total.shape, 1)
        total[...] = jnp.where(pixel < side * side, total[...], 0.0)
        for j, (start, _) in enumerate(spans(total.shape[1])):
            write_chunks(outs[j * n : (j + 1) * n], total, me, n, start)


def conv_forward(x, kernel, side, n):
    depth, pixels = x.shape
    wide = lanes_of(pixels + side + 1)
    width = kernel.shape[2]
    parts = [(width // n, stop - start) for start, stop in spans(wide) for _ in range(n)]
    outs = pl.pallas_call(
        functools.partial(conv_forward_body, side=side, n=n),
        out_shape=[like(part) for part in parts],
        grid=(3,),
        in_specs=[
            whole((depth, pixels)),
            pl.BlockSpec((3, depth, width), lambda t: (t, 0, 0)),
        ],
        out_specs=[whole(part) for part in parts],
        scratch_shapes=[
            pltpu.VMEM((3, depth, wide), BF16),
            pltpu.VMEM((3 * depth, wide), BF16),
            pltpu.VMEM((width, wide), F32),
        ],
        compiler_params=params(),
        cost_estimate=cost(2 * TAPS * depth * width * wide, 2 * kernel.size + 4 * x.size),
    )(x, kernel)
    return outs[:n], outs[n:]


def conv_back_body(m_ref, w_ref, *refs, side, n):
    outs, padded, (planes, total) = refs[:n], refs[n], refs[n + 1 :]
    t = pl.program_id(0)
    me = lax.axis_index("cout")

    @pl.when(t == 0)
    def _():
        fill_columns(planes, m_ref[...], side)
        padded[...] = planes[1]
        total[...] = jnp.zeros_like(total)

    term = None
    for k in range(3):
        part = dot(w_ref[k], read_shifted(planes, 1 - t, 1 - k, side), NN)
        term = part if term is None else term + part
    total[...] += term

    @pl.when(t == 2)
    def _():
        write_chunks(outs, total, me, n)


def conv_back(m, kernel, side, n):
    width, pixels = m.shape
    wide = lanes_of(pixels + side + 1)
    depth = kernel.shape[1]
    outs = pl.pallas_call(
        functools.partial(conv_back_body, side=side, n=n),
        out_shape=[like((depth // n, pixels))] * n + [like((width, wide))],
        grid=(3,),
        in_specs=[
            whole((width, pixels)),
            pl.BlockSpec((3, depth, width), lambda t: (t, 0, 0)),
        ],
        out_specs=[whole((depth // n, pixels))] * n + [whole((width, wide))],
        scratch_shapes=[
            pltpu.VMEM((3, width, wide), BF16),
            pltpu.VMEM((depth, wide), F32),
        ],
        compiler_params=params(),
        cost_estimate=cost(2 * TAPS * depth * width * wide, 2 * kernel.size + 4 * width * wide),
    )(m, kernel)
    return outs[:n], outs[n]


def conv_weight_body(xa_ref, xb_ref, ma_ref, mb_ref, o_ref, pa, pb, both, *, side):
    t = pl.program_id(0)
    wide = pa.shape[2]

    @pl.when(t == 0)
    def _():
        fill_columns(pa, xa_ref[...], side)
        fill_columns(pb, xb_ref[...], side)
        both[:, :wide] = ma_ref[...]
        both[:, wide:] = mb_ref[...]

    dy, dx = t // 3 - 1, t % 3 - 1
    window = jnp.concatenate(
        [read_shifted(pa, dy, dx, side), read_shifted(pb, dy, dx, side)], axis=1
    )
    o_ref[0] = dot(window, both[...], NT)


def conv_weight(xa, xb, ma, mb, side):
    depth, pixels = xa.shape
    width, wide = ma.shape
    return pl.pallas_call(
        functools.partial(conv_weight_body, side=side),
        out_shape=like((TAPS, depth, width), F32),
        grid=(TAPS,),
        in_specs=[whole((depth, pixels))] * 2 + [whole((width, wide))] * 2,
        out_specs=pl.BlockSpec((1, depth, width), lambda t: (t, 0, 0)),
        scratch_shapes=[pltpu.VMEM((3, depth, wide), BF16)] * 2
        + [pltpu.VMEM((width, 2 * wide), BF16)],
        compiler_params=params(),
        cost_estimate=cost(4 * TAPS * depth * width * wide, 4 * TAPS * depth * width),
    )(xa, xb, ma, mb)


def fill_moved(moved, cots, half):
    count, rows, pixels = cots.shape
    wide = moved.shape[2] // count
    column = lax.broadcasted_iota(jnp.int32, (rows, wide), 1) % half
    for b in range(count):
        moved[0, :, b * wide : (b + 1) * wide] = jnp.zeros((rows, wide), moved.dtype)
        moved[0, :, b * wide : b * wide + pixels] = cots[b]
        image = moved[0, :, b * wide : (b + 1) * wide]
        inner = jnp.where(column == 0, jnp.zeros_like(image), image)
        moved[1, :, b * wide : (b + 1) * wide] = pltpu.roll(inner, wide - 1, 1)
        moved[2, :, b * wide : (b + 1) * wide] = pltpu.roll(image, wide - half, 1)
        moved[3, :, b * wide : (b + 1) * wide] = pltpu.roll(inner, wide - half - 1, 1)


def chosen(plane, small, large, side):
    half = side // 2
    i = lax.broadcasted_iota(jnp.int32, (small, large), 0)
    q = lax.broadcasted_iota(jnp.int32, (small, large), 1)
    row, column = i // half, i % half
    pixel = (2 * row + plane // 2) * side + 2 * column + plane % 2
    hit = (q == pixel) & (i < half * half)
    return jnp.where(hit, 1.0, 0.0).astype(BF16)


def half_back_body(g_ref, w_ref, kept, sent, moved, total, placed, *, side):
    t = pl.program_id(0)
    count = g_ref.shape[0]
    rows, pixels = placed.shape
    half = rows // 2
    wide = moved.shape[2] // count
    core = lax.axis_index("section")

    @pl.when(t == 0)
    def _():
        fill_moved(moved, g_ref[...], side // 2)
        total[...] = jnp.zeros_like(total)

    ty, tx = t // 3, t % 3
    plane = jnp.where(ty == 1, 0, 2) + jnp.where(tx == 1, 0, 1)
    move = jnp.where(ty == 0, 2, 0) + jnp.where(tx == 0, 1, 0)
    total[plane] += dot(w_ref[0], moved[move], NN)

    @pl.when(t == TAPS - 1)
    def _():
        for b in range(count):
            for k in range(4):
                term = dot(
                    total[k, :, b * wide : (b + 1) * wide].astype(BF16),
                    chosen(k, wide, pixels, side),
                    NN,
                )
                placed[...] = term if k == 0 else placed[...] + term
            kept[b * half : (b + 1) * half, :] = placed[rows_at(core, half), :].astype(BF16)
            sent[b * half : (b + 1) * half, :] = placed[rows_at(1 - core, half), :].astype(BF16)


def half_back(cots, kernel, side):
    count, width, small = cots.shape
    depth = kernel.shape[1]
    wide = lanes_of(small + side // 2 + 1)
    pixels = lanes_of(side * side + side + 1)
    out = (count * depth // 2, pixels)
    return pl.pallas_call(
        functools.partial(half_back_body, side=side),
        out_shape=[like(out)] * 2,
        grid=(TAPS,),
        in_specs=[
            whole((count, width, small)),
            pl.BlockSpec((1, depth, width), lambda t: (t, 0, 0)),
        ],
        out_specs=[whole(out)] * 2,
        scratch_shapes=[
            pltpu.VMEM((4, width, count * wide), BF16),
            pltpu.VMEM((4, depth, count * wide), F32),
            pltpu.VMEM((depth, pixels), F32),
        ],
        compiler_params=params(),
        cost_estimate=cost(2 * TAPS * depth * width * count * small * 2, 2 * kernel.size),
    )(cots, kernel)


def half_weight_body(*refs, side):
    mine, other, g_ref, o_ref, (moved, planes) = refs[0:2], refs[2:4], refs[4], refs[5], refs[6:]
    t = pl.program_id(0)
    count = g_ref.shape[0]
    half = mine[0].shape[0] // count
    pixels = sum(ref.shape[1] for ref in mine)
    wide = moved.shape[2] // count
    core = lax.axis_index("section")

    @pl.when(t == 0)
    def _():
        fill_moved(moved, g_ref[...], side // 2)
        for k in range(4):
            pick = chosen(k, wide, pixels, side)
            for pair, place in ((mine, core), (other, 1 - core)):
                for b in range(count):
                    rows = slice(b * half, (b + 1) * half)
                    plane = None
                    for ref, (start, stop) in zip(pair, spans(pixels)):
                        term = dot(ref[rows, :], pick[:, start:stop], NT)
                        plane = term if plane is None else plane + term
                    planes[k, rows_at(place, half), b * wide : (b + 1) * wide] = plane.astype(BF16)

    ty, tx = t // 3, t % 3
    plane = jnp.where(ty == 1, 0, 2) + jnp.where(tx == 1, 0, 1)
    move = jnp.where(ty == 0, 2, 0) + jnp.where(tx == 0, 1, 0)
    o_ref[0] = dot(planes[plane], moved[move], NT)


def half_weight(mine, other, cots, side):
    count, width, small = cots.shape
    depth = 2 * mine[0].shape[0] // count
    wide = lanes_of(small + side // 2 + 1)
    return pl.pallas_call(
        functools.partial(half_weight_body, side=side),
        out_shape=like((TAPS, depth, width), F32),
        grid=(TAPS,),
        in_specs=[whole(v.shape) for v in (*mine, *other, cots)],
        out_specs=pl.BlockSpec((1, depth, width), lambda t: (t, 0, 0)),
        scratch_shapes=[
            pltpu.VMEM((4, width, count * wide), BF16),
            pltpu.VMEM((4, depth, count * wide), BF16),
        ],
        compiler_params=params(),
        cost_estimate=cost(
            2 * TAPS * depth * width * count * small * 2, 4 * TAPS * depth * width
        ),
    )(*mine, *other, cots)


def expand(first_block, weight, n):
    depth, width = weight.shape
    pixels = first_block.shape[1]

    def body(x_ref, w_ref, *rest):
        outs, total = rest[:n], rest[n]
        total[...] = dot(w_ref[...], x_ref[...], TN)
        write_chunks(outs, total, lax.axis_index("cout"), n)

    return one_step(
        body,
        [first_block, weight],
        [like((width // n, pixels))] * n,
        [pltpu.VMEM((width, pixels), F32)],
        2 * depth * width * pixels,
    )


def round_target(r, core, z, n):
    return z // (n // 2), z ^ r ^ (core * (n // 2))


def round_block(r, core, z, n):
    place = z ^ r
    return lax.rem(place, n // 2), core ^ (place // (n // 2))


def round_pairs(r, n, back):
    pairs = []
    for core in range(2):
        for z in range(n):
            to_core, to_z = round_target(r, core, z, n)
            pair = (core * n + z, to_core * n + to_z)
            pairs.append(pair[::-1] if back else pair)
    return pairs


def round_send(value, r, n, back=False):
    return lax.ppermute(value, ("section", "cout"), round_pairs(r, n, back))


def reduce_forward(parts, weight, n):
    size, pixels = parts[0].shape
    depth, width = weight.shape
    half = width // 2

    def body(*refs):
        ins, w_ref = refs[:n], refs[n]
        joined, kept, sent, total = refs[n + 1 :]
        core, z = lax.axis_index("section"), lax.axis_index("cout")
        for r in range(n):
            block, image = round_block(r, core, z, n)
            joined[image, rows_at(block, size), :] = ins[r][...]
        for image in range(2):
            total[...] = dot(w_ref[...], joined[image], TN)
            span = slice(image * half, (image + 1) * half)
            kept[span, :] = total[rows_at(core, half), :].astype(BF16)
            sent[span, :] = total[rows_at(1 - core, half), :].astype(BF16)

    return one_step(
        body,
        [*parts, weight],
        [like((2, depth, pixels)), like((2 * half, pixels)), like((2 * half, pixels))],
        [pltpu.VMEM((width, pixels), F32)],
        4 * depth * width * pixels,
    )


def add_halves(kept, got, n):
    rows, pixels = kept.shape
    size = rows // 2 // n

    def body(a_ref, b_ref, *rest):
        outs, total = rest[:n], rest[n]
        me = lax.axis_index("cin")
        total[...] = a_ref[...].astype(F32) + b_ref[...].astype(F32)
        for k in range(n):
            for image in range(2):
                start = image * (rows // 2) + partner(me, k, n) * size
                value = total[pl.ds(pl.multiple_of(start, 8), size), :]
                outs[k][image * size : (image + 1) * size, :] = value.astype(BF16)

    return one_step(
        body,
        [kept, got],
        [like((2 * size, pixels))] * n,
        [pltpu.VMEM((rows, pixels), F32)],
        rows * pixels,
    )


def join_pieces(parts, n):
    double, pixels = parts[0].shape
    size = double // 2

    def body(*refs):
        ins, out, held = refs[:n], refs[n], refs[n + 1]
        me = lax.axis_index("cin")
        for k in range(n):
            for image in range(2):
                start = image * n * size + source(me, k, n) * size
                value = ins[k][image * size : (image + 1) * size, :]
                held[pl.ds(pl.multiple_of(start, 8), size), :] = value.astype(held.dtype)
        out[...] = held[...].astype(BF16)

    return one_step(
        body,
        parts,
        [like((n * double, pixels))],
        [pltpu.VMEM((n * double, pixels), held_type(size))],
        double * pixels,
    )[0]


def place_halves(masked, mine, other, core):
    half = mine.shape[0] // 2
    for image in range(2):
        rows = slice(image * half, (image + 1) * half)
        masked[image, rows_at(core, half), :] = mine[rows, :]
        masked[image, rows_at(1 - core, half), :] = other[rows, :]


def reduce_back(mine, other, weight, n):
    depth, width = weight.shape
    pixels = mine.shape[1]
    size = depth // (n // 2)

    def body(*refs):
        a, b, w_ref = refs[:3]
        outs, masked = refs[3 : 3 + n], refs[3 + n]
        core, z = lax.axis_index("section"), lax.axis_index("cout")
        place_halves(masked, a, b, core)
        for r in range(n):
            block, image = round_block(r, core, z, n)
            outs[r][...] = dot(w_ref[rows_at(block, size), :], masked[image], NN).astype(BF16)

    return one_step(
        body,
        [mine, other, weight],
        [like((size, pixels))] * n,
        [pltpu.VMEM((2, width, pixels), BF16)],
        4 * depth * width * pixels,
    )


def reduce_weight_gradient(joined, mine, other):
    _, depth, _ = joined[0].shape
    width = mine[0].shape[0]
    pixels = sum(v.shape[1] for v in mine)

    def body(*refs):
        js, a, b, out = refs[0:2], refs[2:4], refs[4:6], refs[6]
        core = lax.axis_index("section")
        for j in range(2):
            masked = refs[7 + j]
            place_halves(masked, a[j], b[j], core)
            term = dot(js[j][0], masked[0], NT) + dot(js[j][1], masked[1], NT)
            out[...] = term if j == 0 else out[...] + term

    return one_step(
        body,
        [*joined, *mine, *other],
        [like((depth, width), F32)],
        [pltpu.VMEM((2, width, v.shape[1]), BF16) for v in mine],
        4 * depth * width * pixels,
    )[0]


def expand_back(parts, weight, m, n):
    size, pixels = parts[0].shape
    depth, width = weight.shape

    def body(*refs):
        ins, w_ref, outs = refs[:n], refs[n], refs[n + 1 : n + 1 + m]
        held, total = refs[n + 1 + m :]
        z = lax.axis_index("cout")
        for k in range(n):
            held[rows_at(source(z, k, n), size), :] = ins[k][...]
        total[...] = dot(w_ref[...], held[...], NN)
        write_chunks(outs, total, lax.axis_index("cin"), m)

    outs = one_step(
        body,
        [*parts, weight],
        [like((depth // m, pixels))] * m + [like((width, pixels))],
        [pltpu.VMEM((depth, pixels), F32)],
        2 * depth * width * pixels,
    )
    return outs[:m], outs[m]


def outer_sum(lefts, rights):
    depth, width = lefts[0].shape[0], rights[0].shape[0]
    count = len(lefts)

    def body(*refs):
        a, b, out = refs[:count], refs[count : 2 * count], refs[2 * count]
        for j in range(count):
            term = dot(a[j][...], b[j][...], NT)
            out[...] = term if j == 0 else out[...] + term

    return one_step(
        body,
        [*lefts, *rights],
        [like((depth, width), F32)],
        [],
        2 * width * sum(v.size for v in lefts),
    )[0]


def axis_size(name):
    return lax.axis_size(name)


def swap(value):
    return lax.ppermute(value, "section", [(0, 1), (1, 0)])


def after(value, *earlier):
    return lax.optimization_barrier((value, earlier))[0]


def exchange(parts, name):
    n = len(parts)
    return [parts[0]] + [
        lax.ppermute(parts[k], name, [(i, partner(i, k, n)) for i in range(n)])
        for k in range(1, n)
    ]


def spread(shard, name):
    return exchange([shard] * axis_size(name), name)


def add_up(parts):
    total = parts[0].astype(F32)
    for part in parts[1:]:
        total = total + part.astype(F32)
    return total


def turn(images):
    return jnp.transpose(images, (0, 2, 1))


def collect(shard, name, axis):
    n = axis_size(name)
    me = lax.axis_index(name)
    size = shard.shape[axis]
    shape = shard.shape[:axis] + (n * size,) + shard.shape[axis + 1 :]
    filled = lax.dynamic_update_slice_in_dim(jnp.zeros(shape, shard.dtype), shard, me * size, axis)
    for k in range(1, n):
        got = lax.ppermute(shard, name, [(i, partner(i, k, n)) for i in range(n)])
        filled = lax.dynamic_update_slice_in_dim(filled, got, source(me, k, n) * size, axis)
    return filled


def gather(shard, name):
    return lax.all_gather(shard, name, axis=0, tiled=True)


def both_blocks(
    inner_features,
    block_input,
    first_kernel,
    expand_weight,
    reduce_weight,
    stride_kernel,
    output_grad,
):
    m, n = axis_size("cin"), axis_size("cout")
    pixels = SIDE * SIDE
    wide = lanes_of(pixels + SIDE + 1)
    cuts = spans(wide)
    skip = jnp.pad(turn(block_input)[0], ((0, 0), (0, wide - pixels)))
    cots = turn(output_grad)

    feature_block = gather(turn(inner_features)[0], "cout")
    first_parts = conv_forward(feature_block, first_kernel, SIDE, m)
    cot_block = collect(after(cots, first_parts), "cout", 1)
    first_got = []
    for j in range(2):
        first_got.append(exchange(first_parts[j], "cin"))

    hidden, first_block, expand_got = [], [], []
    ready = None
    for j in range(2):
        got = first_got[j] if j == 0 else after(first_got[j], ready)
        hidden.append(add_up(got))
        act = smooth_gate(hidden[j]).astype(BF16)
        first_block.append(gather(act, "cin"))
        ready = expand(first_block[j], expand_weight, n)
        expand_got.append(exchange(ready, "cout"))

    back_kept, back_sent = half_back(after(cot_block, ready), stride_kernel, SIDE)
    feature_other = swap(after(feature_block, ready))
    first_other = [swap(after(v, ready)) for v in first_block]

    joined_pre, joined_got = [], []
    for j in range(2):
        start, stop = cuts[j]
        got = after(expand_got[j], back_kept)
        joined_pre.append(skip[:, start:stop].astype(F32) + add_up(got))
        joined = smooth_gate(joined_pre[j]).astype(BF16)
        joined_got.append([round_send(joined, r, n) for r in range(n)])
    back_other = swap(back_sent)
    back_parts = add_halves(back_kept, back_other, m)
    back_got = exchange(back_parts, "cin")

    joined_two, hidden_got = [], []
    for j in range(2):
        got = after(joined_got[j], back_parts)
        if j > 0:
            got = after(got, parts, feature_other, first_other)
        two, kept, sent = reduce_forward(got, reduce_weight, n)
        joined_two.append(two)
        other_sent = swap(sent)
        parts = add_halves(kept, other_sent, m)
        hidden_got.append(exchange(parts, "cin"))
    back_piece = add_up(back_got)
    act_piece, mine, other, round_got = [], [], [], []
    for j in range(2):
        start, stop = cuts[j]
        got = hidden_got[j] if j == 0 else after(hidden_got[j], ready)
        piece = add_up(got)
        act_piece.append(smooth_gate(piece).astype(BF16))
        masked = (back_piece[:, start:stop] * gate_slope(piece)).astype(BF16)
        mask_got = spread(masked, "cin")
        if j == 0:
            mask_got = after(mask_got, parts)
        mine.append(join_pieces(mask_got, m))
        other.append(swap(mine[j]))
        ready = reduce_back(mine[j], other[j], reduce_weight, n)
        round_got.append([round_send(ready[r], r, n, True) for r in range(n)])
    act_got = [spread(v, "cin") for v in after(act_piece, ready)]

    input_gradient, input_got = [], []
    for j in range(2):
        slope = gate_slope(joined_pre[j])
        got = after(round_got[0], ready) if j == 0 else after(round_got[1], act_mine)
        input_gradient.append((add_up(got) * slope).astype(BF16))
        input_got.append(spread(input_gradient[j], "cout"))
        if j > 0:
            break
        reduce_gradient = reduce_weight_gradient(after(joined_two, input_gradient[0]), mine, other)
        act_got = after(act_got, reduce_gradient)
        act_mine = [join_pieces(v, m) for v in act_got]
    act_other = [swap(v) for v in act_mine]
    stride_gradient = half_weight(act_mine, act_other, cot_block, SIDE)

    input_wide, back_got = [], []
    for j in range(2):
        got = after(input_got[j], stride_gradient, *input_wide)
        parts, block = expand_back(got, expand_weight, m, n)
        input_wide.append(block)
        back_got.append(exchange(parts, "cin"))
    input_other = [swap(v) for v in after(input_wide, parts)]
    expand_gradient = outer_sum([*first_block, *first_other], [*input_wide, *input_other])
    masked_first = []
    for j in range(2):
        got = after(back_got[j], expand_gradient)
        masked_first.append((add_up(got) * gate_slope(hidden[j])).astype(BF16))
    masked_block = gather(jnp.concatenate(masked_first, axis=1)[:, :pixels], "cin")
    inner_parts, padded = conv_back(masked_block, first_kernel, SIDE, n)
    inner_got = exchange(inner_parts, "cout")
    padded_other = swap(padded)
    first_gradient = conv_weight(feature_block, feature_other, padded, padded_other, SIDE)
    inner_gradient = add_up(after(inner_got, first_gradient))
    outward = jnp.concatenate(input_gradient, axis=1)[:, :pixels]
    return (
        turn(inner_gradient[None]),
        turn(outward[None]),
        first_gradient,
        expand_gradient,
        reduce_gradient,
        stride_gradient,
    )


def solution(mesh):
    return jax.shard_map(
        both_blocks,
        mesh=mesh,
        in_specs=(
            P("section", None, ("cin", "cout")),
            P("section", None, ("cin", "cout")),
            P(None, "cin", "cout"),
            P("cout", "cin"),
            P(("cin", "section"), "cout"),
            P(None, "cout", ("section", "cin")),
            P(None, None, ("section", "cin", "cout")),
        ),
        out_specs=(
            P("section", None, ("cin", "cout")),
            P("section", None, ("cin", "cout")),
            P(None, "cin", "cout"),
            P("cout", "cin"),
            P(("cin", "section"), "cout"),
            P(None, "cout", ("section", "cin")),
        ),
        check_vma=False,
    )
```

```python
import functools

import jax
import jax.numpy as jnp
from jax import lax
from jax.experimental import pallas as pl
from jax.experimental.pallas import tpu as pltpu
from jax.sharding import PartitionSpec as P

SIDE = 28
TAPS = 9
F32 = jnp.float32
BF16 = jnp.bfloat16
NN = (((1,), (0,)), ((), ()))
TN = (((0,), (0,)), ((), ()))
NT = (((1,), (1,)), ((), ()))


def smooth_gate(values):
    return values * jax.nn.sigmoid(values)


def gate_slope(values):
    logistic = jax.nn.sigmoid(values)
    return logistic * (1.0 + values * (1.0 - logistic))


def dot(left, right, dims):
    return lax.dot_general(left, right, dims, preferred_element_type=F32)


def lanes_of(count):
    return -(-count // 128) * 128


def params():
    return pltpu.CompilerParams(
        dimension_semantics=("arbitrary",), vmem_limit_bytes=56 * 1024 * 1024
    )


def cost(flops, moved):
    return pl.CostEstimate(flops=flops, bytes_accessed=moved, transcendentals=0)


def fill_columns(planes, image, side):
    column = lax.broadcasted_iota(jnp.int32, image.shape, 1) % side
    zero = jnp.zeros_like(image)
    span = image.shape[1]
    planes[0, :, :span] = jnp.where(column == side - 1, zero, image)
    planes[1, :, :span] = image
    planes[2, :, :span] = jnp.where(column == 0, zero, image)
    if planes.shape[2] > span:
        for k in range(3):
            planes[k, :, span:] = jnp.zeros((image.shape[0], planes.shape[2] - span), image.dtype)


def read_shifted(planes, dy, dx, side):
    wide = planes.shape[2]
    amount = (2 * wide - (side * dy + dx)) % wide
    return pltpu.roll(planes[dx + 1], amount, 1)


def partner(index, k, n):
    return index ^ k if n & (n - 1) == 0 else (index + k) % n


def source(index, k, n):
    return index ^ k if n & (n - 1) == 0 else (index + n - k) % n


def whole(shape):
    return pl.BlockSpec(shape, lambda *_: (0,) * len(shape))


def one_step(body, ins, outs, scratch, flops):
    moved = sum(v.size * v.dtype.itemsize for v in ins)
    moved += sum(v.size * v.dtype.itemsize for v in outs)
    return pl.pallas_call(
        body,
        out_shape=outs,
        in_specs=[pl.BlockSpec(memory_space=pltpu.VMEM)] * len(ins),
        out_specs=[pl.BlockSpec(memory_space=pltpu.VMEM)] * len(outs),
        scratch_shapes=scratch,
        compiler_params=pltpu.CompilerParams(vmem_limit_bytes=56 * 1024 * 1024),
        cost_estimate=cost(flops, moved),
    )(*ins)


def like(shape, dtype=BF16):
    return jax.ShapeDtypeStruct(shape, dtype)


def held_type(size):
    return BF16 if size % 16 == 0 else F32


def rows_at(index, size):
    return pl.ds(pl.multiple_of(index * size, 8), size)


def write_chunks(outs, total, me, n, start=0):
    size, width = outs[0].shape
    for k in range(n):
        rows = rows_at(partner(me, k, n), size)
        outs[k][...] = total[rows, start : start + width].astype(BF16)


def spans(wide):
    first = wide // 256 * 128
    return ((0, first), (first, wide))


def stack_row(windows, planes, dy, step, side):
    depth = planes.shape[1]
    for k in range(3):
        windows[k * depth : (k + 1) * depth, :] = read_shifted(planes, dy, step * (k - 1), side)


def conv_forward_body(x_ref, w_ref, *rest, side, n):
    outs, (planes, windows, total) = rest[:-3], rest[-3:]
    t = pl.program_id(0)
    me = lax.axis_index("cin")

    @pl.when(t == 0)
    def _():
        fill_columns(planes, x_ref[...], side)
        total[...] = jnp.zeros_like(total)

    stack_row(windows, planes, t - 1, 1, side)
    total[...] += dot(w_ref[...].reshape(windows.shape[0], w_ref.shape[2]), windows[...], TN)

    @pl.when(t == 2)
    def _():
        pixel = lax.broadcasted_iota(jnp.int32, total.shape, 1)
        total[...] = jnp.where(pixel < side * side, total[...], 0.0)
        for j, (start, _) in enumerate(spans(total.shape[1])):
            write_chunks(outs[j * n : (j + 1) * n], total, me, n, start)


def conv_forward(x, kernel, side, n):
    depth, pixels = x.shape
    wide = lanes_of(pixels + side + 1)
    width = kernel.shape[2]
    parts = [(width // n, stop - start) for start, stop in spans(wide) for _ in range(n)]
    outs = pl.pallas_call(
        functools.partial(conv_forward_body, side=side, n=n),
        out_shape=[like(part) for part in parts],
        grid=(3,),
        in_specs=[
            whole((depth, pixels)),
            pl.BlockSpec((3, depth, width), lambda t: (t, 0, 0)),
        ],
        out_specs=[whole(part) for part in parts],
        scratch_shapes=[
            pltpu.VMEM((3, depth, wide), BF16),
            pltpu.VMEM((3 * depth, wide), BF16),
            pltpu.VMEM((width, wide), F32),
        ],
        compiler_params=params(),
        cost_estimate=cost(2 * TAPS * depth * width * wide, 2 * kernel.size + 4 * x.size),
    )(x, kernel)
    return outs[:n], outs[n:]


def conv_back_body(m_ref, w_ref, *refs, side, n):
    outs, (planes, total) = refs[:n], refs[n:]
    t = pl.program_id(0)
    me = lax.axis_index("cout")

    @pl.when(t == 0)
    def _():
        fill_columns(planes, m_ref[...], side)
        total[...] = jnp.zeros_like(total)

    term = None
    for k in range(3):
        part = dot(w_ref[k], read_shifted(planes, 1 - t, 1 - k, side), NN)
        term = part if term is None else term + part
    total[...] += term

    @pl.when(t == 2)
    def _():
        write_chunks(outs, total, me, n)


def conv_back(m, kernel, side, n):
    width, pixels = m.shape
    wide = lanes_of(pixels + side + 1)
    depth = kernel.shape[1]
    return pl.pallas_call(
        functools.partial(conv_back_body, side=side, n=n),
        out_shape=[like((depth // n, pixels))] * n,
        grid=(3,),
        in_specs=[
            whole((width, pixels)),
            pl.BlockSpec((3, depth, width), lambda t: (t, 0, 0)),
        ],
        out_specs=[whole((depth // n, pixels))] * n,
        scratch_shapes=[
            pltpu.VMEM((3, width, wide), BF16),
            pltpu.VMEM((depth, wide), F32),
        ],
        compiler_params=params(),
        cost_estimate=cost(2 * TAPS * depth * width * wide, 2 * kernel.size + 4 * width * wide),
    )(m, kernel)


def conv_weight_body(xa_ref, xb_ref, ma_ref, mb_ref, o_ref, pa, pb, both, *, side):
    t = pl.program_id(0)
    wide, pixels = pa.shape[2], ma_ref.shape[1]

    @pl.when(t == 0)
    def _():
        fill_columns(pa, xa_ref[...], side)
        fill_columns(pb, xb_ref[...], side)
        both[...] = jnp.zeros_like(both)
        both[:, :pixels] = ma_ref[...]
        both[:, wide : wide + pixels] = mb_ref[...]

    dy, dx = t // 3 - 1, t % 3 - 1
    window = jnp.concatenate(
        [read_shifted(pa, dy, dx, side), read_shifted(pb, dy, dx, side)], axis=1
    )
    o_ref[0] = dot(window, both[...], NT)


def conv_weight(xa, xb, ma, mb, side):
    depth, pixels = xa.shape
    width = ma.shape[0]
    wide = lanes_of(pixels + side + 1)
    return pl.pallas_call(
        functools.partial(conv_weight_body, side=side),
        out_shape=like((TAPS, depth, width), F32),
        grid=(TAPS,),
        in_specs=[whole((depth, pixels))] * 2 + [whole((width, pixels))] * 2,
        out_specs=pl.BlockSpec((1, depth, width), lambda t: (t, 0, 0)),
        scratch_shapes=[pltpu.VMEM((3, depth, wide), BF16)] * 2
        + [pltpu.VMEM((width, 2 * wide), BF16)],
        compiler_params=params(),
        cost_estimate=cost(4 * TAPS * depth * width * wide, 4 * TAPS * depth * width),
    )(xa, xb, ma, mb)


def fill_moved(moved, cots, half):
    count, rows, pixels = cots.shape
    wide = moved.shape[2] // count
    column = lax.broadcasted_iota(jnp.int32, (rows, wide), 1) % half
    for b in range(count):
        moved[0, :, b * wide : (b + 1) * wide] = jnp.zeros((rows, wide), moved.dtype)
        moved[0, :, b * wide : b * wide + pixels] = cots[b]
        image = moved[0, :, b * wide : (b + 1) * wide]
        inner = jnp.where(column == 0, jnp.zeros_like(image), image)
        moved[1, :, b * wide : (b + 1) * wide] = pltpu.roll(inner, wide - 1, 1)
        moved[2, :, b * wide : (b + 1) * wide] = pltpu.roll(image, wide - half, 1)
        moved[3, :, b * wide : (b + 1) * wide] = pltpu.roll(inner, wide - half - 1, 1)


def chosen(plane, small, large, side):
    half = side // 2
    i = lax.broadcasted_iota(jnp.int32, (small, large), 0)
    q = lax.broadcasted_iota(jnp.int32, (small, large), 1)
    row, column = i // half, i % half
    pixel = (2 * row + plane // 2) * side + 2 * column + plane % 2
    hit = (q == pixel) & (i < half * half)
    return jnp.where(hit, 1.0, 0.0).astype(BF16)


def half_back_body(g_ref, w_ref, kept, sent, moved, total, placed, *, side):
    t = pl.program_id(0)
    count = g_ref.shape[0]
    rows, pixels = placed.shape
    half = rows // 2
    wide = moved.shape[2] // count
    core = lax.axis_index("section")

    @pl.when(t == 0)
    def _():
        fill_moved(moved, g_ref[...], side // 2)
        total[...] = jnp.zeros_like(total)

    ty, tx = t // 3, t % 3
    plane = jnp.where(ty == 1, 0, 2) + jnp.where(tx == 1, 0, 1)
    move = jnp.where(ty == 0, 2, 0) + jnp.where(tx == 0, 1, 0)
    total[plane] += dot(w_ref[0], moved[move], NN)

    @pl.when(t == TAPS - 1)
    def _():
        for b in range(count):
            for k in range(4):
                term = dot(
                    total[k, :, b * wide : (b + 1) * wide].astype(BF16),
                    chosen(k, wide, pixels, side),
                    NN,
                )
                placed[...] = term if k == 0 else placed[...] + term
            kept[b * half : (b + 1) * half, :] = placed[rows_at(core, half), :].astype(BF16)
            sent[b * half : (b + 1) * half, :] = placed[rows_at(1 - core, half), :].astype(BF16)


def half_back(cots, kernel, side):
    count, width, small = cots.shape
    depth = kernel.shape[1]
    wide = lanes_of(small + side // 2 + 1)
    pixels = lanes_of(side * side + side + 1)
    out = (count * depth // 2, pixels)
    return pl.pallas_call(
        functools.partial(half_back_body, side=side),
        out_shape=[like(out)] * 2,
        grid=(TAPS,),
        in_specs=[
            whole((count, width, small)),
            pl.BlockSpec((1, depth, width), lambda t: (t, 0, 0)),
        ],
        out_specs=[whole(out)] * 2,
        scratch_shapes=[
            pltpu.VMEM((4, width, count * wide), BF16),
            pltpu.VMEM((4, depth, count * wide), F32),
            pltpu.VMEM((depth, pixels), F32),
        ],
        compiler_params=params(),
        cost_estimate=cost(2 * TAPS * depth * width * count * small * 2, 2 * kernel.size),
    )(cots, kernel)


def half_weight_body(*refs, side):
    mine, other, g_ref, o_ref, moved, planes = refs
    t = pl.program_id(0)
    count = g_ref.shape[0]
    half = mine.shape[0] // count
    pixels = mine.shape[1]
    wide = moved.shape[2] // count
    core = lax.axis_index("section")

    @pl.when(t == 0)
    def _():
        fill_moved(moved, g_ref[...], side // 2)
        for k in range(4):
            pick = chosen(k, wide, pixels, side)
            for ref, place in ((mine, core), (other, 1 - core)):
                for b in range(count):
                    plane = dot(ref[b * half : (b + 1) * half, :], pick, NT)
                    planes[k, rows_at(place, half), b * wide : (b + 1) * wide] = plane.astype(BF16)

    ty, tx = t // 3, t % 3
    plane = jnp.where(ty == 1, 0, 2) + jnp.where(tx == 1, 0, 1)
    move = jnp.where(ty == 0, 2, 0) + jnp.where(tx == 0, 1, 0)
    o_ref[0] = dot(planes[plane], moved[move], NT)


def half_weight(mine, other, cots, side):
    count, width, small = cots.shape
    depth = 2 * mine.shape[0] // count
    wide = lanes_of(small + side // 2 + 1)
    return pl.pallas_call(
        functools.partial(half_weight_body, side=side),
        out_shape=like((TAPS, depth, width), F32),
        grid=(TAPS,),
        in_specs=[whole(v.shape) for v in (mine, other, cots)],
        out_specs=pl.BlockSpec((1, depth, width), lambda t: (t, 0, 0)),
        scratch_shapes=[
            pltpu.VMEM((4, width, count * wide), BF16),
            pltpu.VMEM((4, depth, count * wide), BF16),
        ],
        compiler_params=params(),
        cost_estimate=cost(
            2 * TAPS * depth * width * count * small * 2, 4 * TAPS * depth * width
        ),
    )(mine, other, cots)


def expand(first_block, weight, n):
    depth, width = weight.shape
    pixels = first_block.shape[1]

    def body(x_ref, w_ref, *rest):
        outs, total = rest[:n], rest[n]
        total[...] = dot(w_ref[...], x_ref[...], TN)
        write_chunks(outs, total, lax.axis_index("cout"), n)

    return one_step(
        body,
        [first_block, weight],
        [like((width // n, pixels))] * n,
        [pltpu.VMEM((width, pixels), F32)],
        2 * depth * width * pixels,
    )


def round_target(r, core, z, n):
    return z // (n // 2), z ^ r ^ (core * (n // 2))


def round_block(r, core, z, n):
    place = z ^ r
    return lax.rem(place, n // 2), core ^ (place // (n // 2))


def round_pairs(r, n, back):
    pairs = []
    for core in range(2):
        for z in range(n):
            to_core, to_z = round_target(r, core, z, n)
            pair = (core * n + z, to_core * n + to_z)
            pairs.append(pair[::-1] if back else pair)
    return pairs


def round_send(value, r, n, back=False):
    return lax.ppermute(value, ("section", "cout"), round_pairs(r, n, back))


def reduce_forward(parts, weight, n):
    size, pixels = parts[0].shape
    depth, width = weight.shape
    half = width // 2

    def body(*refs):
        ins, w_ref = refs[:n], refs[n]
        joined, kept, sent, total = refs[n + 1 :]
        core, z = lax.axis_index("section"), lax.axis_index("cout")
        for r in range(n):
            block, image = round_block(r, core, z, n)
            joined[image, rows_at(block, size), :] = ins[r][...]
        for image in range(2):
            total[...] = dot(w_ref[...], joined[image], TN)
            span = slice(image * half, (image + 1) * half)
            kept[span, :] = total[rows_at(core, half), :].astype(BF16)
            sent[span, :] = total[rows_at(1 - core, half), :].astype(BF16)

    return one_step(
        body,
        [*parts, weight],
        [like((2, depth, pixels)), like((2 * half, pixels)), like((2 * half, pixels))],
        [pltpu.VMEM((width, pixels), F32)],
        4 * depth * width * pixels,
    )


def add_halves(kept, got, n):
    rows, pixels = kept.shape
    size = rows // 2 // n

    def body(a_ref, b_ref, *rest):
        outs, total = rest[:n], rest[n]
        me = lax.axis_index("cin")
        total[...] = a_ref[...].astype(F32) + b_ref[...].astype(F32)
        for k in range(n):
            for image in range(2):
                start = image * (rows // 2) + partner(me, k, n) * size
                value = total[pl.ds(pl.multiple_of(start, 8), size), :]
                outs[k][image * size : (image + 1) * size, :] = value.astype(BF16)

    return one_step(
        body,
        [kept, got],
        [like((2 * size, pixels))] * n,
        [pltpu.VMEM((rows, pixels), F32)],
        rows * pixels,
    )


def join_pieces(parts, n):
    double, pixels = parts[0].shape
    size = double // 2

    def body(*refs):
        ins, out, held = refs[:n], refs[n], refs[n + 1]
        me = lax.axis_index("cin")
        for k in range(n):
            for image in range(2):
                start = image * n * size + source(me, k, n) * size
                value = ins[k][image * size : (image + 1) * size, :]
                held[pl.ds(pl.multiple_of(start, 8), size), :] = value.astype(held.dtype)
        out[...] = held[...].astype(BF16)

    return one_step(
        body,
        parts,
        [like((n * double, pixels))],
        [pltpu.VMEM((n * double, pixels), held_type(size))],
        double * pixels,
    )[0]


def place_halves(masked, mine, other, core):
    half = mine.shape[0] // 2
    for image in range(2):
        rows = slice(image * half, (image + 1) * half)
        masked[image, rows_at(core, half), :] = mine[rows, :]
        masked[image, rows_at(1 - core, half), :] = other[rows, :]


def reduce_back(mine, other, weight, n):
    depth, width = weight.shape
    pixels = mine.shape[1]
    size = depth // (n // 2)

    def body(*refs):
        a, b, w_ref = refs[:3]
        outs, masked = refs[3 : 3 + n], refs[3 + n]
        core, z = lax.axis_index("section"), lax.axis_index("cout")
        place_halves(masked, a, b, core)
        for r in range(n):
            block, image = round_block(r, core, z, n)
            outs[r][...] = dot(w_ref[rows_at(block, size), :], masked[image], NN).astype(BF16)

    return one_step(
        body,
        [mine, other, weight],
        [like((size, pixels))] * n,
        [pltpu.VMEM((2, width, pixels), BF16)],
        4 * depth * width * pixels,
    )


def reduce_weight_gradient(joined, mine, other):
    _, depth, _ = joined[0].shape
    width = mine[0].shape[0]
    pixels = sum(v.shape[1] for v in mine)

    def body(*refs):
        js, a, b, out = refs[0:2], refs[2:4], refs[4:6], refs[6]
        core = lax.axis_index("section")
        for j in range(2):
            masked = refs[7 + j]
            place_halves(masked, a[j], b[j], core)
            term = dot(js[j][0], masked[0], NT) + dot(js[j][1], masked[1], NT)
            out[...] = term if j == 0 else out[...] + term

    return one_step(
        body,
        [*joined, *mine, *other],
        [like((depth, width), F32)],
        [pltpu.VMEM((2, width, v.shape[1]), BF16) for v in mine],
        4 * depth * width * pixels,
    )[0]


def expand_back(parts, weight, m, n):
    size, pixels = parts[0].shape
    depth, width = weight.shape

    def body(*refs):
        ins, w_ref, outs = refs[:n], refs[n], refs[n + 1 : n + 1 + m]
        held, total = refs[n + 1 + m :]
        z = lax.axis_index("cout")
        for k in range(n):
            held[rows_at(source(z, k, n), size), :] = ins[k][...]
        total[...] = dot(w_ref[...], held[...], NN)
        write_chunks(outs, total, lax.axis_index("cin"), m)

    outs = one_step(
        body,
        [*parts, weight],
        [like((depth // m, pixels))] * m + [like((width, pixels))],
        [pltpu.VMEM((depth, pixels), F32)],
        2 * depth * width * pixels,
    )
    return outs[:m], outs[m]


def outer_sum(lefts, rights):
    depth, width = lefts[0].shape[0], rights[0].shape[0]
    count = len(lefts)

    def body(*refs):
        a, b, out = refs[:count], refs[count : 2 * count], refs[2 * count]
        for j in range(count):
            term = dot(a[j][...], b[j][...], NT)
            out[...] = term if j == 0 else out[...] + term

    return one_step(
        body,
        [*lefts, *rights],
        [like((depth, width), F32)],
        [],
        2 * width * sum(v.size for v in lefts),
    )[0]


def axis_size(name):
    return lax.axis_size(name)


def swap(value):
    return lax.ppermute(value, "section", [(0, 1), (1, 0)])


def swap_blocks(value, n):
    rows, width = value.shape
    return swap(value.reshape(n, rows // n, width)).reshape(rows, width)


def after(value, *earlier):
    return lax.optimization_barrier((value, earlier))[0]


def exchange(parts, name):
    n = len(parts)
    return [parts[0]] + [
        lax.ppermute(parts[k], name, [(i, partner(i, k, n)) for i in range(n)])
        for k in range(1, n)
    ]


def spread(shard, name):
    return exchange([shard] * axis_size(name), name)


def add_up(parts):
    total = parts[0].astype(F32)
    for part in parts[1:]:
        total = total + part.astype(F32)
    return total


def turn(images):
    return jnp.transpose(images, (0, 2, 1))


def collect(shard, name, axis):
    n = axis_size(name)
    me = lax.axis_index(name)
    size = shard.shape[axis]
    shape = shard.shape[:axis] + (n * size,) + shard.shape[axis + 1 :]
    filled = lax.dynamic_update_slice_in_dim(jnp.zeros(shape, shard.dtype), shard, me * size, axis)
    for k in range(1, n):
        got = lax.ppermute(shard, name, [(i, partner(i, k, n)) for i in range(n)])
        filled = lax.dynamic_update_slice_in_dim(filled, got, source(me, k, n) * size, axis)
    return filled


def gather(shard, name):
    return lax.all_gather(shard, name, axis=0, tiled=True)


def both_blocks(
    inner_features,
    block_input,
    first_kernel,
    expand_weight,
    reduce_weight,
    stride_kernel,
    output_grad,
):
    m, n = axis_size("cin"), axis_size("cout")
    pixels = SIDE * SIDE
    wide = lanes_of(pixels + SIDE + 1)
    cuts = spans(wide)
    skip = jnp.pad(turn(block_input)[0], ((0, 0), (0, wide - pixels)))
    cots = turn(output_grad)

    feature_block = gather(turn(inner_features)[0], "cout")
    first_parts = conv_forward(feature_block, first_kernel, SIDE, m)
    cot_block = collect(after(cots, first_parts), "cout", 1)
    first_got = []
    for j in range(2):
        first_got.append(exchange(first_parts[j], "cin"))

    hidden, first_block, expand_got = [], [], []
    ready = None
    for j in range(2):
        got = first_got[j] if j == 0 else after(first_got[j], ready)
        hidden.append(add_up(got))
        act = smooth_gate(hidden[j]).astype(BF16)
        first_block.append(gather(act, "cin"))
        ready = expand(first_block[j], expand_weight, n)
        expand_got.append(exchange(ready, "cout"))

    back_kept, back_sent = half_back(after(cot_block, ready), stride_kernel, SIDE)
    feature_other = swap_blocks(after(feature_block, ready), n)
    first_other = [swap(after(v, ready)) for v in first_block]

    joined_pre, joined_got = [], []
    for j in range(2):
        start, stop = cuts[j]
        got = after(expand_got[j], back_kept)
        joined_pre.append(skip[:, start:stop].astype(F32) + add_up(got))
        joined = smooth_gate(joined_pre[j]).astype(BF16)
        joined_got.append([round_send(joined, r, n) for r in range(n)])
    back_other = swap(back_sent)
    back_parts = add_halves(back_kept, back_other, m)
    back_got = exchange(back_parts, "cin")

    joined_two, hidden_got = [], []
    for j in range(2):
        got = after(joined_got[j], back_parts)
        if j > 0:
            got = after(got, parts, feature_other, first_other)
        two, kept, sent = reduce_forward(got, reduce_weight, n)
        joined_two.append(two)
        other_sent = swap(sent)
        parts = add_halves(kept, other_sent, m)
        hidden_got.append(exchange(parts, "cin"))
    back_piece = add_up(back_got)
    act_piece, mine, other, round_got = [], [], [], []
    for j in range(2):
        start, stop = cuts[j]
        got = hidden_got[j] if j == 0 else after(hidden_got[j], ready)
        piece = add_up(got)
        act_piece.append(smooth_gate(piece).astype(BF16))
        masked = (back_piece[:, start:stop] * gate_slope(piece)).astype(BF16)
        mask_got = spread(masked, "cin")
        if j == 0:
            mask_got = after(mask_got, parts)
        mine.append(join_pieces(mask_got, m))
        other.append(swap(mine[j]))
        if j > 0:
            act_got = spread(jnp.concatenate(act_piece, axis=1), "cin")
        ready = reduce_back(mine[j], other[j], reduce_weight, n)
        round_got.append([round_send(ready[r], r, n, True) for r in range(n)])
    input_gradient, input_got = [], []
    input_wide, input_other, back_got = [], [], []
    for j in range(2):
        slope = gate_slope(joined_pre[j])
        input_gradient.append((add_up(round_got[j]) * slope).astype(BF16))
        input_got.append(spread(input_gradient[j], "cout"))
        got = input_got[j]
        if j > 0:
            stride_gradient = half_weight(act_mine, act_other, cot_block, SIDE)
            got = after(got, stride_gradient)
        parts, block = expand_back(got, expand_weight, m, n)
        input_wide.append(block)
        back_got.append(exchange(parts, "cin"))
        input_other.append(swap(block))
        if j > 0:
            break
        reduce_gradient = reduce_weight_gradient(after(joined_two, ready), mine, other)
        act_mine = join_pieces(after(act_got, reduce_gradient), m)
        act_other = swap(act_mine)
        round_got[1] = after(round_got[1], act_mine)
    expand_gradient = outer_sum([*first_block, *first_other], [*input_wide, *input_other])
    masked_first = []
    for j in range(2):
        got = after(back_got[j], expand_gradient)
        masked_first.append((add_up(got) * gate_slope(hidden[j])).astype(BF16))
    masked_block = gather(jnp.concatenate(masked_first, axis=1)[:, :pixels], "cin")
    masked_other = swap_blocks(masked_block, m)
    inner_parts = conv_back(masked_block, first_kernel, SIDE, n)
    inner_got = exchange(inner_parts, "cout")
    first_gradient = conv_weight(
        feature_block, feature_other, masked_block, masked_other, SIDE
    )
    inner_gradient = add_up(after(inner_got, first_gradient))
    outward = jnp.concatenate(input_gradient, axis=1)[:, :pixels]
    return (
        turn(inner_gradient[None]),
        turn(outward[None]),
        first_gradient,
        expand_gradient,
        reduce_gradient,
        stride_gradient,
    )


def solution(mesh):
    return jax.shard_map(
        both_blocks,
        mesh=mesh,
        in_specs=(
            P("section", None, ("cin", "cout")),
            P("section", None, ("cin", "cout")),
            P(None, "cin", "cout"),
            P("cout", "cin"),
            P(("cin", "section"), "cout"),
            P(None, "cout", ("section", "cin")),
            P(None, None, ("section", "cin", "cout")),
        ),
        out_specs=(
            P("section", None, ("cin", "cout")),
            P("section", None, ("cin", "cout")),
            P(None, "cin", "cout"),
            P("cout", "cin"),
            P(("cin", "section"), "cout"),
            P(None, "cout", ("section", "cin")),
        ),
        check_vma=False,
    )
```

```python
import functools

import jax
import jax.numpy as jnp
from jax import lax
from jax.experimental import pallas as pl
from jax.experimental.pallas import tpu as pltpu
from jax.sharding import PartitionSpec as P

SIDE = 28
TAPS = 9
CORES, CIN, COUT = "section", "cin", "cout"
F32 = jnp.float32
BF16 = jnp.bfloat16
NN = (((1,), (0,)), ((), ()))
TN = (((0,), (0,)), ((), ()))
NT = (((1,), (1,)), ((), ()))


def smooth_gate(values):
    return values * jax.nn.sigmoid(values)


def gate_slope(values):
    logistic = jax.nn.sigmoid(values)
    return logistic * (1.0 + values * (1.0 - logistic))


def dot(left, right, dims):
    return lax.dot_general(left, right, dims, preferred_element_type=F32)


def lanes_of(count):
    return -(-count // 128) * 128


def params():
    return pltpu.CompilerParams(
        vmem_limit_bytes=56 * 1024 * 1024
    )


def cost(flops, moved):
    return pl.CostEstimate(flops=flops, bytes_accessed=moved, transcendentals=0)


def fill_columns(planes, image, side):
    column = lax.broadcasted_iota(jnp.int32, image.shape, 1) % side
    zero = jnp.zeros_like(image)
    span = image.shape[1]
    planes[0, :, :span] = jnp.where(column == side - 1, zero, image)
    planes[1, :, :span] = image
    planes[2, :, :span] = jnp.where(column == 0, zero, image)
    if planes.shape[2] > span:
        for k in range(3):
            planes[k, :, span:] = jnp.zeros((image.shape[0], planes.shape[2] - span), image.dtype)


def read_shifted(planes, dy, dx, side):
    wide = planes.shape[2]
    amount = (2 * wide - (side * dy + dx)) % wide
    return pltpu.roll(planes[dx + 1], amount, 1)


def partner(index, k, n):
    return index ^ k if n & (n - 1) == 0 else (index + k) % n


def source(index, k, n):
    return index ^ k if n & (n - 1) == 0 else (index + n - k) % n


def whole(shape):
    return pl.BlockSpec(shape, lambda *_: (0,) * len(shape))


def one_step(body, ins, outs, scratch, flops):
    moved = sum(v.size * v.dtype.itemsize for v in ins)
    moved += sum(v.size * v.dtype.itemsize for v in outs)
    return pl.pallas_call(
        body,
        out_shape=outs,
        in_specs=[pl.BlockSpec(memory_space=pltpu.VMEM)] * len(ins),
        out_specs=[pl.BlockSpec(memory_space=pltpu.VMEM)] * len(outs),
        scratch_shapes=scratch,
        compiler_params=pltpu.CompilerParams(vmem_limit_bytes=56 * 1024 * 1024),
        cost_estimate=cost(flops, moved),
    )(*ins)


def like(shape, dtype=BF16):
    return jax.ShapeDtypeStruct(shape, dtype)


def rows_at(index, size):
    return pl.ds(pl.multiple_of(index * size, 8), size)


def write_chunks(outs, total, me, n, start=0):
    size, width = outs[0].shape
    for k in range(n):
        rows = rows_at(partner(me, k, n), size)
        outs[k][...] = total[rows, start : start + width].astype(BF16)


def spans(wide):
    first = wide // 256 * 128
    return ((0, first), (first, wide))


def stack_row(windows, planes, dy, step, side):
    depth = planes.shape[1]
    for k in range(3):
        windows[k * depth : (k + 1) * depth, :] = read_shifted(planes, dy, step * (k - 1), side)


def conv_forward_body(x_ref, w_ref, *rest, side, n):
    outs, (planes, windows, total) = rest[:-3], rest[-3:]
    t = pl.program_id(0)
    me = lax.axis_index(CIN)

    @pl.when(t == 0)
    def _():
        fill_columns(planes, x_ref[...], side)
        total[...] = jnp.zeros_like(total)

    stack_row(windows, planes, t - 1, 1, side)
    total[...] += dot(w_ref[...].reshape(windows.shape[0], w_ref.shape[2]), windows[...], TN)

    @pl.when(t == 2)
    def _():
        pixel = lax.broadcasted_iota(jnp.int32, total.shape, 1)
        total[...] = jnp.where(pixel < side * side, total[...], 0.0)
        for j, (start, _) in enumerate(spans(total.shape[1])):
            write_chunks(outs[j * n : (j + 1) * n], total, me, n, start)


def conv_forward(x, kernel, side, n):
    depth, pixels = x.shape
    wide = lanes_of(pixels + side + 1)
    width = kernel.shape[2]
    parts = [(width // n, stop - start) for start, stop in spans(wide) for _ in range(n)]
    outs = pl.pallas_call(
        functools.partial(conv_forward_body, side=side, n=n),
        out_shape=[like(part) for part in parts],
        grid=(3,),
        in_specs=[
            whole((depth, pixels)),
            pl.BlockSpec((3, depth, width), lambda t: (t, 0, 0)),
        ],
        out_specs=[whole(part) for part in parts],
        scratch_shapes=[
            pltpu.VMEM((3, depth, wide), BF16),
            pltpu.VMEM((3 * depth, wide), BF16),
            pltpu.VMEM((width, wide), F32),
        ],
        compiler_params=params(),
        cost_estimate=cost(2 * TAPS * depth * width * wide, 2 * kernel.size + 4 * x.size),
    )(x, kernel)
    return outs[:n], outs[n:]


def conv_back_body(m_ref, w_ref, *refs, side, n):
    outs, (planes, total) = refs[:n], refs[n:]
    t = pl.program_id(0)
    me = lax.axis_index(COUT)

    @pl.when(t == 0)
    def _():
        fill_columns(planes, m_ref[...], side)
        total[...] = jnp.zeros_like(total)

    term = None
    for k in range(3):
        part = dot(w_ref[k], read_shifted(planes, 1 - t, 1 - k, side), NN)
        term = part if term is None else term + part
    total[...] += term

    @pl.when(t == 2)
    def _():
        write_chunks(outs, total, me, n)


def conv_back(m, kernel, side, n):
    width, pixels = m.shape
    wide = lanes_of(pixels + side + 1)
    depth = kernel.shape[1]
    return pl.pallas_call(
        functools.partial(conv_back_body, side=side, n=n),
        out_shape=[like((depth // n, pixels))] * n,
        grid=(3,),
        in_specs=[
            whole((width, pixels)),
            pl.BlockSpec((3, depth, width), lambda t: (t, 0, 0)),
        ],
        out_specs=[whole((depth // n, pixels))] * n,
        scratch_shapes=[
            pltpu.VMEM((3, width, wide), BF16),
            pltpu.VMEM((depth, wide), F32),
        ],
        compiler_params=params(),
        cost_estimate=cost(2 * TAPS * depth * width * wide, 2 * kernel.size + 4 * width * wide),
    )(m, kernel)


def conv_weight_body(xa_ref, xb_ref, ma_ref, mb_ref, o_ref, pa, pb, both, *, side):
    t = pl.program_id(0)
    wide, pixels = pa.shape[2], ma_ref.shape[1]

    @pl.when(t == 0)
    def _():
        fill_columns(pa, xa_ref[...], side)
        fill_columns(pb, xb_ref[...], side)
        both[...] = jnp.zeros_like(both)
        both[:, :pixels] = ma_ref[...]
        both[:, wide : wide + pixels] = mb_ref[...]

    dy, dx = t // 3 - 1, t % 3 - 1
    window = jnp.concatenate(
        [read_shifted(pa, dy, dx, side), read_shifted(pb, dy, dx, side)], axis=1
    )
    o_ref[0] = dot(window, both[...], NT)


def conv_weight(xa, xb, ma, mb, side):
    depth, pixels = xa.shape
    width = ma.shape[0]
    wide = lanes_of(pixels + side + 1)
    return pl.pallas_call(
        functools.partial(conv_weight_body, side=side),
        out_shape=like((TAPS, depth, width), F32),
        grid=(TAPS,),
        in_specs=[whole((depth, pixels))] * 2 + [whole((width, pixels))] * 2,
        out_specs=pl.BlockSpec((1, depth, width), lambda t: (t, 0, 0)),
        scratch_shapes=[pltpu.VMEM((3, depth, wide), BF16)] * 2
        + [pltpu.VMEM((width, 2 * wide), BF16)],
        compiler_params=params(),
        cost_estimate=cost(4 * TAPS * depth * width * wide, 4 * TAPS * depth * width),
    )(xa, xb, ma, mb)


def fill_moved(moved, images, half):
    count = len(images)
    rows, pixels = images[0].shape
    wide = moved.shape[2] // count
    column = lax.broadcasted_iota(jnp.int32, (rows, wide), 1) % half
    for b in range(count):
        moved[0, :, b * wide : (b + 1) * wide] = jnp.zeros((rows, wide), moved.dtype)
        moved[0, :, b * wide : b * wide + pixels] = images[b]
        image = moved[0, :, b * wide : (b + 1) * wide]
        inner = jnp.where(column == 0, jnp.zeros_like(image), image)
        moved[1, :, b * wide : (b + 1) * wide] = pltpu.roll(inner, wide - 1, 1)
        moved[2, :, b * wide : (b + 1) * wide] = pltpu.roll(image, wide - half, 1)
        moved[3, :, b * wide : (b + 1) * wide] = pltpu.roll(inner, wide - half - 1, 1)


def chosen(plane, small, large, side):
    half = side // 2
    i = lax.broadcasted_iota(jnp.int32, (small, large), 0)
    q = lax.broadcasted_iota(jnp.int32, (small, large), 1)
    row, column = i // half, i % half
    pixel = (2 * row + plane // 2) * side + 2 * column + plane % 2
    hit = (q == pixel) & (i < half * half)
    return jnp.where(hit, 1.0, 0.0).astype(BF16)


def half_back_body(g_ref, w_ref, kept, sent, moved, total, placed, *, side):
    t = pl.program_id(0)
    count = g_ref.shape[0]
    pixels = placed.shape[1]
    wide = moved.shape[2] // count
    core = lax.axis_index(CORES)

    @pl.when(t == 0)
    def _():
        fill_moved(moved, [g_ref[core], g_ref[1 - core]], side // 2)
        total[...] = jnp.zeros_like(total)

    ty, tx = t // 3, t % 3
    plane = jnp.where(ty == 1, 0, 2) + jnp.where(tx == 1, 0, 1)
    move = jnp.where(ty == 0, 2, 0) + jnp.where(tx == 0, 1, 0)
    total[plane] += dot(w_ref[0], moved[move], NN)

    @pl.when(t == TAPS - 1)
    def _():
        for b in range(count):
            for k in range(4):
                term = dot(
                    total[k, :, b * wide : (b + 1) * wide].astype(BF16),
                    chosen(k, wide, pixels, side),
                    NN,
                )
                placed[...] = term if k == 0 else placed[...] + term
            (kept, sent)[b][...] = placed[...].astype(BF16)


def half_back(cots, kernel, side):
    count, width, small = cots.shape
    depth = kernel.shape[1]
    wide = lanes_of(small + side // 2 + 1)
    pixels = lanes_of(side * side + side + 1)
    out = (depth, pixels)
    return pl.pallas_call(
        functools.partial(half_back_body, side=side),
        out_shape=[like(out)] * 2,
        grid=(TAPS,),
        in_specs=[
            whole((count, width, small)),
            pl.BlockSpec((1, depth, width), lambda t: (t, 0, 0)),
        ],
        out_specs=[whole(out)] * 2,
        scratch_shapes=[
            pltpu.VMEM((4, width, count * wide), BF16),
            pltpu.VMEM((4, depth, count * wide), F32),
            pltpu.VMEM((depth, pixels), F32),
        ],
        compiler_params=params(),
        cost_estimate=cost(2 * TAPS * depth * width * count * small * 2, 2 * kernel.size),
    )(cots, kernel)


def half_weight_body(*refs, side):
    mine, other, g_ref, o_ref, moved, planes = refs
    t = pl.program_id(0)
    count = g_ref.shape[0]
    pixels = mine.shape[1]
    wide = moved.shape[2] // count
    core = lax.axis_index(CORES)

    @pl.when(t == 0)
    def _():
        fill_moved(moved, [g_ref[core], g_ref[1 - core]], side // 2)
        for k in range(4):
            pick = chosen(k, wide, pixels, side)
            for b, ref in enumerate((mine, other)):
                plane = dot(ref[...], pick, NT)
                planes[k, :, b * wide : (b + 1) * wide] = plane.astype(BF16)

    ty, tx = t // 3, t % 3
    plane = jnp.where(ty == 1, 0, 2) + jnp.where(tx == 1, 0, 1)
    move = jnp.where(ty == 0, 2, 0) + jnp.where(tx == 0, 1, 0)
    o_ref[0] = dot(planes[plane], moved[move], NT)


def half_weight(mine, other, cots, side):
    count, width, small = cots.shape
    depth = mine.shape[0]
    wide = lanes_of(small + side // 2 + 1)
    return pl.pallas_call(
        functools.partial(half_weight_body, side=side),
        out_shape=like((TAPS, depth, width), F32),
        grid=(TAPS,),
        in_specs=[whole(v.shape) for v in (mine, other, cots)],
        out_specs=pl.BlockSpec((1, depth, width), lambda t: (t, 0, 0)),
        scratch_shapes=[
            pltpu.VMEM((4, width, count * wide), BF16),
            pltpu.VMEM((4, depth, count * wide), BF16),
        ],
        compiler_params=params(),
        cost_estimate=cost(
            2 * TAPS * depth * width * count * small * 2, 4 * TAPS * depth * width
        ),
    )(mine, other, cots)


def expand(first_block, weight, n):
    depth, width = weight.shape
    pixels = first_block.shape[1]

    def body(x_ref, w_ref, *rest):
        outs, total = rest[:n], rest[n]
        total[...] = dot(w_ref[...], x_ref[...], TN)
        write_chunks(outs, total, lax.axis_index(COUT), n)

    return one_step(
        body,
        [first_block, weight],
        [like((width // n, pixels))] * n,
        [pltpu.VMEM((width, pixels), F32)],
        2 * depth * width * pixels,
    )


def reduce_forward(parts, mine, other, n, m):
    size, pixels = parts[0].shape
    depth, width = mine.shape

    def body(*refs):
        ins, a_ref, b_ref = refs[:n], refs[n], refs[n + 1]
        joined, lent, outs, total = refs[n + 2], refs[n + 3], refs[n + 4 : -1], refs[-1]
        core, z = lax.axis_index(CORES), lax.axis_index(COUT)
        for k in range(n):
            joined[rows_at(source(z, k, n), size), :] = ins[k][...]
        lent[...] = joined[rows_at(1 - core, depth), :]
        total[...] = dot(a_ref[...], joined[rows_at(core, depth), :], TN) + dot(
            b_ref[...], lent[...], TN
        )
        write_chunks(outs, total, lax.axis_index(CIN), m)

    outs = one_step(
        body,
        [*parts, mine, other],
        [like((2 * depth, pixels)), like((depth, pixels))] + [like((width // m, pixels))] * m,
        [pltpu.VMEM((width, pixels), F32)],
        4 * depth * width * pixels,
    )
    return outs[0], outs[1], outs[2:]


def add_halves(kept, got, n):
    rows, pixels = kept.shape

    def body(a_ref, b_ref, *rest):
        outs, total = rest[:n], rest[n]
        total[...] = a_ref[...].astype(F32) + b_ref[...].astype(F32)
        write_chunks(outs, total, lax.axis_index(CIN), n)

    return one_step(
        body,
        [kept, got],
        [like((rows // n, pixels))] * n,
        [pltpu.VMEM((rows, pixels), F32)],
        rows * pixels,
    )


def join_pieces(parts, n):
    size, pixels = parts[0].shape

    def body(*refs):
        ins, out = refs[:n], refs[n]
        me = lax.axis_index(CIN)
        for k in range(n):
            out[rows_at(source(me, k, n), size), :] = ins[k][...]

    return one_step(body, parts, [like((n * size, pixels))], [], size * pixels)[0]


def reduce_back(parts, mine, other, m, n):
    size, pixels = parts[0].shape
    depth, width = mine.shape

    def body(*refs):
        ins, a_ref, b_ref = refs[:m], refs[m], refs[m + 1]
        masked, outs, total = refs[m + 2], refs[m + 3 : -1], refs[-1]
        core, c = lax.axis_index(CORES), lax.axis_index(CIN)
        for k in range(m):
            masked[rows_at(source(c, k, m), size), :] = ins[k][...]
        total[rows_at(core, depth), :] = dot(a_ref[...], masked[...], NN)
        total[rows_at(1 - core, depth), :] = dot(b_ref[...], masked[...], NN)
        write_chunks(outs, total, lax.axis_index(COUT), n)

    outs = one_step(
        body,
        [*parts, mine, other],
        [like((width, pixels))] + [like((2 * depth // n, pixels))] * n,
        [pltpu.VMEM((2 * depth, pixels), F32)],
        4 * depth * width * pixels,
    )
    return outs[0], outs[1:]


def reduce_weight_gradient(joined, lent, masked, masked_other):
    depth, width = lent[0].shape[0], masked[0].shape[0]
    count = len(joined)

    def body(*refs):
        out, core = refs[4 * count], lax.axis_index(CORES)
        for j in range(count):
            own, theirs, a, b = refs[j : 4 * count : count]
            term = dot(own[rows_at(core, depth), :], a[...], NT) + dot(theirs[...], b[...], NT)
            out[...] = term if j == 0 else out[...] + term

    return one_step(
        body,
        [*joined, *lent, *masked, *masked_other],
        [like((depth, width), F32)],
        [],
        4 * width * sum(v.size for v in lent),
    )[0]


def expand_back(parts, weight, m, n):
    size, pixels = parts[0].shape
    depth, width = weight.shape

    def body(*refs):
        ins, w_ref, outs = refs[:n], refs[n], refs[n + 1 : n + 1 + m]
        held, total = refs[n + 1 + m :]
        z = lax.axis_index(COUT)
        for k in range(n):
            held[rows_at(source(z, k, n), size), :] = ins[k][...]
        total[...] = dot(w_ref[...], held[...], NN)
        write_chunks(outs, total, lax.axis_index(CIN), m)

    outs = one_step(
        body,
        [*parts, weight],
        [like((depth // m, pixels))] * m + [like((width, pixels))],
        [pltpu.VMEM((depth, pixels), F32)],
        2 * depth * width * pixels,
    )
    return outs[:m], outs[m]


def outer_sum(lefts, rights):
    depth, width = lefts[0].shape[0], rights[0].shape[0]
    count = len(lefts)

    def body(*refs):
        a, b, out = refs[:count], refs[count : 2 * count], refs[2 * count]
        for j in range(count):
            term = dot(a[j][...], b[j][...], NT)
            out[...] = term if j == 0 else out[...] + term

    return one_step(
        body,
        [*lefts, *rights],
        [like((depth, width), F32)],
        [],
        2 * width * sum(v.size for v in lefts),
    )[0]


def axis_size(name):
    return lax.axis_size(name)


def swap(value):
    return lax.ppermute(value, CORES, [(0, 1), (1, 0)])


def swap_blocks(value, n):
    rows, width = value.shape
    return swap(value.reshape(n, rows // n, width)).reshape(rows, width)


def after(value, *earlier):
    return lax.optimization_barrier((value, earlier))[0]


def exchange(parts, name):
    n = len(parts)
    return [parts[0]] + [
        lax.ppermute(parts[k], name, [(i, partner(i, k, n)) for i in range(n)])
        for k in range(1, n)
    ]


def spread(shard, name):
    return exchange([shard] * axis_size(name), name)


def add_up(parts):
    total = parts[0].astype(F32)
    for part in parts[1:]:
        total = total + part.astype(F32)
    return total


def turn(images):
    return jnp.transpose(images, (0, 2, 1))


def collect(shard, name, axis):
    n = axis_size(name)
    me = lax.axis_index(name)
    size = shard.shape[axis]
    shape = shard.shape[:axis] + (n * size,) + shard.shape[axis + 1 :]
    filled = lax.dynamic_update_slice_in_dim(jnp.zeros(shape, shard.dtype), shard, me * size, axis)
    for k in range(1, n):
        got = lax.ppermute(shard, name, [(i, partner(i, k, n)) for i in range(n)])
        filled = lax.dynamic_update_slice_in_dim(filled, got, source(me, k, n) * size, axis)
    return filled


def gather(shard, name):
    return lax.all_gather(shard, name, axis=0, tiled=True)


def both_blocks(
    inner_features,
    block_input,
    first_kernel,
    expand_weight,
    reduce_weight,
    stride_kernel,
    output_grad,
):
    m, n = axis_size(CIN), axis_size(COUT)
    pixels = SIDE * SIDE
    wide = lanes_of(pixels + SIDE + 1)
    cuts = spans(wide)
    skip = jnp.pad(turn(block_input)[0], ((0, 0), (0, wide - pixels)))
    cots = turn(output_grad)

    feature_block = gather(turn(inner_features)[0], COUT)
    first_parts = conv_forward(feature_block, first_kernel, SIDE, m)
    cot_block = collect(after(cots, first_parts), COUT, 1)
    first_got = []
    for j in range(2):
        first_got.append(exchange(first_parts[j], CIN))

    hidden, first_block, expand_got = [], [], []
    ready = None
    for j in range(2):
        got = first_got[j] if j == 0 else after(first_got[j], ready)
        hidden.append(add_up(got))
        act = smooth_gate(hidden[j]).astype(BF16)
        first_block.append(gather(act, CIN))
        ready = expand(first_block[j], expand_weight, n)
        expand_got.append(exchange(ready, COUT))

    back_kept, back_sent = half_back(after(cot_block, ready), stride_kernel, SIDE)
    feature_other = swap_blocks(after(feature_block, ready), n)
    first_other = [swap(after(v, ready)) for v in first_block]
    reduce_other = swap(after(reduce_weight, ready))

    joined_pre, joined_got = [], []
    for j in range(2):
        start, stop = cuts[j]
        got = after(expand_got[j], back_kept)
        joined_pre.append(skip[:, start:stop].astype(F32) + add_up(got))
        joined = smooth_gate(joined_pre[j]).astype(BF16)
        joined_got.append(spread(joined, COUT))
    back_other = swap(back_sent)
    back_parts = add_halves(back_kept, back_other, m)
    back_got = exchange(back_parts, CIN)

    joined_own, joined_lent, hidden_got = [], [], []
    for j in range(2):
        got = after(joined_got[j], back_parts)
        if j > 0:
            got = after(got, parts, feature_other, first_other)
        own, lent, parts = reduce_forward(got, reduce_weight, reduce_other, n, m)
        joined_own.append(own)
        hidden_got.append(exchange(parts, CIN))
        joined_lent.append(lent)
    back_piece = add_up(back_got)
    act_piece, masked, masked_other, round_got = [], [], [], []
    for j in range(2):
        start, stop = cuts[j]
        got = hidden_got[j] if j == 0 else after(hidden_got[j], ready)
        piece = add_up(got)
        act_piece.append(smooth_gate(piece).astype(BF16))
        mask = (back_piece[:, start:stop] * gate_slope(piece)).astype(BF16)
        mask_got = spread(mask, CIN)
        if j == 0:
            mask_got = after(mask_got, parts)
        else:
            act_got = spread(jnp.concatenate(act_piece, axis=1), CIN)
        block, ready = reduce_back(mask_got, reduce_weight, reduce_other, m, n)
        masked.append(block)
        round_got.append(exchange(ready, COUT))
        masked_other.append(swap(block))
        joined_lent[j] = swap(after(joined_lent[j], block))

    input_gradient, input_got = [], []
    input_wide, input_other, back_got = [], [], []
    for j in range(2):
        slope = gate_slope(joined_pre[j])
        input_gradient.append((add_up(round_got[j]) * slope).astype(BF16))
        input_got.append(spread(input_gradient[j], COUT))
        got = input_got[j]
        if j > 0:
            stride_gradient = half_weight(act_mine, act_other, cot_block, SIDE)
            got = after(got, stride_gradient)
        parts, block = expand_back(got, expand_weight, m, n)
        input_wide.append(block)
        back_got.append(exchange(parts, CIN))
        input_other.append(swap(block))
        if j > 0:
            break
        reduce_gradient = reduce_weight_gradient(
            after(joined_own, ready), joined_lent, masked, masked_other
        )
        act_mine = join_pieces(after(act_got, reduce_gradient), m)
        act_other = swap(act_mine)
        round_got[1] = after(round_got[1], act_mine)
    expand_gradient = outer_sum([*first_block, *first_other], [*input_wide, *input_other])
    masked_first = []
    for j in range(2):
        got = after(back_got[j], expand_gradient)
        masked_first.append((add_up(got) * gate_slope(hidden[j])).astype(BF16))
    masked_block = gather(jnp.concatenate(masked_first, axis=1)[:, :pixels], CIN)
    masked_other = swap_blocks(masked_block, m)
    inner_parts = conv_back(masked_block, first_kernel, SIDE, n)
    inner_got = exchange(inner_parts, COUT)
    first_gradient = conv_weight(
        feature_block, feature_other, masked_block, masked_other, SIDE
    )
    inner_gradient = add_up(after(inner_got, first_gradient))
    outward = jnp.concatenate(input_gradient, axis=1)[:, :pixels]
    return (
        turn(inner_gradient[None]),
        turn(outward[None]),
        first_gradient,
        expand_gradient,
        reduce_gradient,
        stride_gradient,
    )


def solution(mesh):
    return jax.shard_map(
        both_blocks,
        mesh=mesh,
        in_specs=(
            P(CORES, None, (CIN, COUT)),
            P(CORES, None, (CIN, COUT)),
            P(None, CIN, COUT),
            P(COUT, CIN),
            P((CIN, CORES), COUT),
            P(None, COUT, (CORES, CIN)),
            P(None, None, (CORES, CIN, COUT)),
        ),
        out_specs=(
            P(CORES, None, (CIN, COUT)),
            P(CORES, None, (CIN, COUT)),
            P(None, CIN, COUT),
            P(COUT, CIN),
            P((CIN, CORES), COUT),
            P(None, COUT, (CORES, CIN)),
        ),
        check_vma=False,
    )
```
